512 devices in a mesh: feat: 32 (over x, z), tok: 16 (over y, core).
Axes of the slice: x: 4, y: 8, z: 8, core: 2. Of those that a mesh axis runs over, the one named last changes fastest.
Arguments:
- activations: bfloat16 [2048, 8192], P('tok', 'feat'), may hold values from -6 to 6
- w_base: bfloat16 [8192, 8192], P('feat', 'tok'), may hold values from -0.0625 to 0.0625
- blk_vals: bfloat16 [96, 128, 128], P('feat'), may hold values from -0.5 to 0.5
- blk_index: int32 [96, 2], P('feat'), may hold values from 0 to 63, as said below
- blk_count: int32 [32], P('feat'), may hold values from 1 to 3, as said below
- a_down: bfloat16 [8192, 64], P('feat'), may hold values from -0.0625 to 0.0625
- b_up: bfloat16 [64, 8192], P(None, 'feat'), may hold values from -0.75 to 0.75
- grad_out: bfloat16 [2048, 8192], P('tok', 'feat'), may hold values from -6 to 6
Outputs:
- projected: bfloat16 [2048, 8192], P('tok', 'feat')
- grad_x: bfloat16 [2048, 8192], P('tok', 'feat')
- grad_blocks: float32 [96, 128, 128], P('feat')
- grad_a: float32 [8192, 64], P('feat')
- grad_b: float32 [64, 8192], P(None, 'feat')
The draws below stay inside these ranges and needn't reach their ends.
Inputs may be any that keep to these rules, and one draw needn't show every extreme that they name: `blk_index`: column 0 is below 2 and column 1 below 64; both largest values occur in every draw. `blk_count`: some feature shard holds exactly 3 live slots in every draw.
All inputs are finite; a program needn't handle non-finite values.
Results may differ from the reference program's by a relative error of at most 0.014.
Values may be sent and summed in bfloat16 or wider, within the bound.
A program may use at most 64 MiB of HBM per device.

```python
import jax
import jax.numpy as jnp
from jax import lax

D = 8192
RANK = 64
BLK = 128
SLOTS = 3
TOKENS = 2048
SHARDS = 32
RBLK = 2
CBLK = 64
N_FEAT = 32


def draw_blk_index(key, part):
    row_key = jax.random.fold_in(key, 11)
    col_key = jax.random.fold_in(key, 12)
    rows = jax.random.randint(row_key, (SHARDS * SLOTS,), 0, RBLK).astype(jnp.int32)
    cols = jax.random.randint(col_key, (SHARDS * SLOTS,), 0, CBLK).astype(jnp.int32)
    rows = rows.at[0].set(RBLK - 1)
    cols = cols.at[0].set(CBLK - 1)
    return jnp.stack([rows, cols], axis=1)


def draw_blk_count(key, part):
    count_key = jax.random.fold_in(key, 21)
    pick_key = jax.random.fold_in(key, 22)
    counts = jax.random.randint(count_key, (SHARDS,), 1, SLOTS + 1).astype(jnp.int32)
    chosen = jax.random.randint(pick_key, (), 0, SHARDS)
    return counts.at[chosen].set(SLOTS)


def steps_of(key, shape, split, low, high):
    level, own = 1.0, jax.random.fold_in(key, 6)
    for axis_at, parts in split:
        draws = jnp.exp(jax.random.uniform(jax.random.fold_in(own, axis_at), (parts,), jnp.float32, low / len(split), high / len(split)))
        level = level * jnp.repeat(draws, shape[axis_at] // parts).reshape([-1 if axis == axis_at else 1 for axis in range(len(shape))])
    return level


def normal_values(rng, extent, scale, reach, shards=(), held_as=jnp.bfloat16):
    array = jax.random.normal(rng, extent, jnp.float32) * scale
    if len(shards) > 0:
        array = steps_of(rng, extent, shards, -0.22, 0.18) * array
    return jnp.clip(array, min=-reach, max=reach).astype(held_as)


def setup_inputs(seed: int = 0) -> dict:
    streams_of = jax.random.split(jax.random.key(seed), 9)
    return {
        "activations": normal_values(streams_of[0], (TOKENS, D), 1.0, 6.0, ((0, 16), (1, 32))),
        "w_base": normal_values(streams_of[1], (D, D), D ** -0.5, 0.0625, ((0, 32), (1, 16))),
        "blk_vals": normal_values(streams_of[2], (SHARDS * SLOTS, BLK, BLK), BLK ** -0.5, 0.5, ((0, 32),)),
        "blk_index": draw_blk_index(jax.random.fold_in(streams_of[8], 71), 0),
        "blk_count": draw_blk_count(jax.random.fold_in(streams_of[8], 71), 0),
        "a_down": normal_values(streams_of[5], (D, RANK), D ** -0.5, 0.0625, ((0, 32),)),
        "b_up": normal_values(streams_of[6], (RANK, D), RANK ** -0.5, 0.75, ((1, 32),)),
        "grad_out": normal_values(streams_of[7], (TOKENS, D), 1.0, 6.0, ((0, 16), (1, 32))),
    }


def reference(activations, w_base, blk_vals, blk_index, blk_count, a_down, b_up, grad_out):
    tok_rows = activations.shape[0]
    full_width = activations.shape[1]
    shard_width = full_width // N_FEAT
    grad_scale = float(tok_rows) ** -0.5
    backward = jnp.dot(grad_out, w_base.T, preferred_element_type=jnp.float32)
    u_half = jnp.dot(activations, a_down, preferred_element_type=jnp.float32).astype(jnp.bfloat16)
    v_half = jnp.dot(grad_out, b_up.T, preferred_element_type=jnp.float32).astype(jnp.bfloat16)
    summed = jnp.zeros((tok_rows, full_width), jnp.float32)
    block_grads = []
    for owner_idx in range(N_FEAT):
        x_shard = activations[:, owner_idx * shard_width:(owner_idx + 1) * shard_width]
        w_shard = w_base[owner_idx * shard_width:(owner_idx + 1) * shard_width, :]
        partial_value = jnp.dot(x_shard, w_shard, preferred_element_type=jnp.float32)
        for local_idx in range(SLOTS):
            slot_idx = owner_idx * SLOTS + local_idx
            is_live = (local_idx < blk_count[owner_idx]).astype(jnp.float32)
            local_row = (blk_index[slot_idx, 0] * BLK).astype(jnp.int32)
            row_start = (owner_idx * shard_width + blk_index[slot_idx, 0] * BLK).astype(jnp.int32)
            col_start = (blk_index[slot_idx, 1] * BLK).astype(jnp.int32)
            x_cols = lax.dynamic_slice_in_dim(x_shard, local_row, BLK, 1)
            g_cols = lax.dynamic_slice_in_dim(grad_out, col_start, BLK, 1)
            forward_add = jnp.dot(x_cols, blk_vals[slot_idx], preferred_element_type=jnp.float32) * is_live
            current = lax.dynamic_slice_in_dim(partial_value, col_start, BLK, 1)
            partial_value = lax.dynamic_update_slice_in_dim(partial_value, current + forward_add, col_start, 1)
            back_add = jnp.dot(g_cols, blk_vals[slot_idx].T, preferred_element_type=jnp.float32) * is_live
            current = lax.dynamic_slice_in_dim(backward, row_start, BLK, 1)
            backward = lax.dynamic_update_slice_in_dim(backward, current + back_add, row_start, 1)
            block_grads.append(jnp.dot(x_cols.T, g_cols, preferred_element_type=jnp.float32) * is_live * grad_scale)
        summed = summed + partial_value.astype(jnp.bfloat16).astype(jnp.float32)
    projected = (summed + jnp.dot(u_half, b_up, preferred_element_type=jnp.float32)).astype(jnp.bfloat16)
    grad_x = (backward + jnp.dot(v_half, a_down.T, preferred_element_type=jnp.float32)).astype(jnp.bfloat16)
    grad_blocks = jnp.stack(block_grads, axis=0)
    grad_a = jnp.dot(activations.T, v_half, preferred_element_type=jnp.float32) * grad_scale
    grad_b = jnp.dot(u_half.T, grad_out, preferred_element_type=jnp.float32) * grad_scale
    return (projected, grad_x, grad_blocks, grad_a, grad_b)
```

```python
import functools

import jax
import jax.numpy as jnp
from jax import lax
from jax.experimental import pallas as pl
from jax.experimental.pallas import tpu as pltpu
from jax.sharding import PartitionSpec as P

MESH = pl.DeviceIdType.MESH
F32 = jnp.float32
BF16 = jnp.bfloat16
BLK = 128
NC = 2


def dot(a, b, ca, cb):
    return lax.dot_general(a, b, (((ca,), (cb,)), ((), ())), preferred_element_type=F32)


def kernel(
    dims, scale,
    x_ref, w_ref, blk_ref, idx_ref, at_ref, b_ref, g_ref,
    proj_ref, gradx_ref, grada_ref, gradb_ref, gradblk_ref,
    wl, wq, xg, gz, orx, os_, gxr, gxs, gxacc, uvx, uvz, uvt, idxg, bs, br, rss, rsr, agb, ab, gab,
    ring_s, ring_r, fwd_s, fwd_r, x_s, x_r, g_s, g_r, o_s, o_r, q_s, q_r,
    ux_s, ux_r, uz_s, uz_r, id_s, id_r, b_s, b_r, rs_s, rs_r, ag_s, ag_r,
):
    nx, ny, nz = dims
    nq = ny // nx
    nt = ny * NC
    half = ny // 2
    feat, tok = lax.axis_index("feat"), lax.axis_index("tok")
    x, z = feat // nz, feat % nz
    y, c = tok // NC, tok % NC
    zc = (z // 2) % 2
    zq, zh = z // (2 * NC), z % 2
    sib = 1 - c
    hb = x_ref.shape[0]
    pending = []

    def dev(xx, yy, zz, cc):
        return (xx * nz + zz, yy * NC + cc)

    def send(src, dst, s_sem, r_sem, target):
        copy = pltpu.make_async_remote_copy(
            src_ref=src, dst_ref=dst, send_sem=s_sem, recv_sem=r_sem, device_id=target, device_id_type=MESH
        )
        copy.start()
        pending.append((None, copy))

    def send_or_keep(mine, src, dst, s_sem, r_sem, target):
        @pl.when(mine)
        def _():
            pltpu.make_async_copy(src, dst, r_sem).start()

        copy = pltpu.make_async_remote_copy(
            src_ref=src, dst_ref=dst, send_sem=s_sem, recv_sem=r_sem, device_id=target, device_id_type=MESH
        )

        @pl.when(jnp.logical_not(mine))
        def _():
            copy.start()

        pending.append((mine, copy))

    def arrived(dst, sem):
        pltpu.make_async_copy(dst, dst, sem).wait()

    barrier = pltpu.get_barrier_semaphore()
    greeted = 0
    for dx in range(1, nx):
        for cc in range(NC):
            pl.semaphore_signal(barrier, inc=1, device_id=dev((x + dx) % nx, y, z, cc), device_id_type=MESH)
            greeted += 1
    for dz in range(1, nz):
        for cc in range(NC):
            pl.semaphore_signal(barrier, inc=1, device_id=dev(x, y, (z + dz) % nz, cc), device_id_type=MESH)
            greeted += 1
    for dt in range(1, nt):
        pl.semaphore_signal(barrier, inc=1, device_id=(feat, (tok + dt) % nt), device_id_type=MESH)
        greeted += 1

    nsl = blk_ref.shape[0]
    for h in range(2):
        for rr in range(2):
            for hh in range(2):
                r0, c0 = rr * BLK, h * 2 * BLK + hh * BLK
                piece = w_ref[r0:r0 + BLK, c0:c0 + BLK].astype(F32)
                column = (tok * 4 + h * 2 + hh).astype(F32)
                for j in range(nsl):
                    hit = jnp.where(idx_ref[j:j + 1, :] == column, 1.0, 0.0) * jnp.where(
                        idx_ref[4 + j:5 + j, :] == float(rr), 1.0, 0.0
                    )
                    piece = piece + hit * blk_ref[j].astype(F32)
                wl[0, h, r0:r0 + BLK, hh * BLK:(hh + 1) * BLK] = piece.astype(BF16)

    rank = at_ref.shape[0]
    ab[...] = jnp.zeros_like(ab)
    ab[0, 0:rank, :] = at_ref[...]
    ab[1, rank:2 * rank, :] = b_ref[...]
    ab[2, 0:rank, :] = b_ref[...]
    ab[3, rank:2 * rank, :] = at_ref[...]
    uvx[x] = (dot(x_ref[...], ab[0], 1, 1) + dot(g_ref[...], ab[1], 1, 1)).astype(BF16)
    idxg[x] = idx_ref[...]

    pl.semaphore_wait(barrier, greeted)

    last = ny - 2

    def ring_slot(direction, k):
        d, sub = k // 2 + 1, (k + direction) % 2
        return (d if direction == 0 else half + d), d, sub

    def ring_send(direction, k):
        if k > last:
            return
        if k < 2:
            src = wl.at[0, (k + direction) % 2]
        else:
            slot, _, sub = ring_slot(direction, k - 2)
            src = wl.at[slot, sub]
        slot, _, sub = ring_slot(direction, k)
        to = (y + 1) % ny if direction == 0 else (y + ny - 1) % ny
        send(src, wl.at[slot, sub], ring_s.at[direction, k], ring_r.at[direction, k], dev(x, to, z, c))

    def hand_on(slot, sub, yy):
        xx, qq = yy // nq, yy % nq
        send_or_keep(x == xx, wl.at[slot, sub], wq.at[x, qq, sub], fwd_s.at[slot, sub], fwd_r.at[x, qq, sub], dev(xx, y, z, c))

    def ring_step(k):
        for direction in range(2):
            slot, d, sub = ring_slot(direction, k)
            arrived(wl.at[slot, sub], ring_r.at[direction, k])
            ring_send(direction, k + 2)
            yy = (y + ny - d) % ny if direction == 0 else (y + d) % ny
            hand_on(slot, sub, yy)

    for k in range(2):
        for direction in range(2):
            ring_send(direction, k)
    for dx in range(1, nx):
        send(uvx.at[x], uvx.at[x], ux_s.at[dx], ux_r.at[x], dev((x + dx) % nx, y, z, c))
    for dx in range(nx):
        for cc in range(NC):
            own = c == cc if dx == 0 else None
            rows = pl.ds(pl.multiple_of(c * hb, hb), hb)
            args = (x_ref, xg.at[x, rows], x_s.at[dx, cc], x_r.at[x, c], dev((x + dx) % nx, y, z, cc))
            if own is None:
                send(*args)
            else:
                send_or_keep(own, *args)
    for dx in range(1, nx):
        send(idxg.at[x], idxg.at[x], id_s.at[dx], id_r.at[x], dev((x + dx) % nx, y, z, c))
    for dz in range(nz):
        rows = pl.ds(pl.multiple_of(c * hb, hb), hb)
        args = (g_ref, gz.at[zq, zh, rows], g_s.at[dz], g_r.at[zq, zh, c], dev(x, y, (z + dz) % nz, zc))
        if dz:
            send(*args)
        else:
            send_or_keep(c == zc, *args)
    for h in range(2):
        hand_on(0, h, y)

    def low_rank_over_z():
        total = uvx[x].astype(F32)
        for dx in range(1, nx):
            xx = (x + dx) % nx
            arrived(uvx.at[xx], ux_r.at[xx])
            total = total + uvx[xx].astype(F32)
        uvz[z] = total.astype(BF16)
        for dz in range(1, nz):
            send(uvz.at[z], uvz.at[z], uz_s.at[dz], uz_r.at[z], dev(x, y, (z + dz) % nz, c))

    def low_rank_done():
        total = uvz[z].astype(F32)
        for dz in range(1, nz):
            zz = (z + dz) % nz
            arrived(uvz.at[zz], uz_r.at[zz])
            total = total + uvz[zz].astype(F32)
        uvt[...] = total.astype(BF16)

    def blocks_over_x():
        for dx in range(nx):
            xx = (x + dx) % nx
            if dx:
                arrived(idxg.at[xx], id_r.at[xx])
            for cc in range(NC):
                arrived(xg.at[xx, cc * hb:(cc + 1) * hb], x_r.at[xx, cc])
        for qq in range(nq):
            for h in range(2):
                for cc in range(NC):
                    arrived(gz.at[qq, h, cc * hb:(cc + 1) * hb], g_r.at[qq, h, cc])
        for dx in range(nx):
            xx = (x + dx) % nx
            for j in range(nsl):
                col, row = idxg[xx, j:j + 1, :], idxg[xx, 4 + j:5 + j, :]
                picked = jnp.zeros((NC * hb, BLK), BF16)
                for qq in range(nq):
                    for h in range(2):
                        base = (2 * (x * nz + 4 * qq + 2 * c + h)).astype(F32)
                        for hh in range(2):
                            hit = jnp.where(col == base + float(hh), 1.0, 0.0).astype(BF16)
                            picked = picked + gz[qq, h, :, hh * BLK:(hh + 1) * BLK] * hit
                top = jnp.where(row == 0.0, 1.0, 0.0).astype(BF16)
                low = jnp.where(row == 1.0, 1.0, 0.0).astype(BF16)
                xs = xg[xx, :, 0:BLK] * top + xg[xx, :, BLK:2 * BLK] * low
                bs[dx, j * BLK:(j + 1) * BLK, :] = dot(xs, picked, 0, 0).astype(BF16)
            if dx:
                send(bs.at[dx], br.at[x], b_s.at[dx], b_r.at[x], dev(xx, y, z, c))

    ra, rb = 2 * rank // nt, nsl * BLK // nt

    def grads_over_tok():
        uv = uvt[...]
        gab[0:rank] = dot(uv, g_ref[...], 0, 0)[0:rank]
        gab[rank:2 * rank] = dot(uv, x_ref[...], 0, 0)[rank:2 * rank]
        for dx in range(1, nx):
            xx = (x + dx) % nx
            arrived(br.at[xx], b_r.at[xx])
        for tt in range(nt):
            rss[tt, 0:ra, :] = gab[tt * ra:(tt + 1) * ra, 0:BLK]
            rss[tt, ra:2 * ra, :] = gab[tt * ra:(tt + 1) * ra, BLK:2 * BLK]
        blk_sum = bs[0].astype(F32)
        for dx in range(1, nx):
            blk_sum = blk_sum + br[(x + dx) % nx].astype(F32)
        for tt in range(nt):
            rss[tt, 2 * ra:2 * ra + rb, :] = blk_sum[tt * rb:(tt + 1) * rb]
        rsr[tok] = rss[tok]
        for dt in range(1, nt):
            tt = (tok + dt) % nt
            send(rss.at[tt], rsr.at[tok], rs_s.at[dt], rs_r.at[tok], (feat, tt))

    def grads_back():
        total = rsr[tok]
        for dt in range(1, nt):
            tt = (tok + dt) % nt
            arrived(rsr.at[tt], rs_r.at[tt])
            total = total + rsr[tt]
        agb[tok] = total * scale
        for dt in range(1, nt):
            send(agb.at[tok], agb.at[tok], ag_s.at[dt], ag_r.at[tok], (feat, (tok + dt) % nt))

    side = [low_rank_over_z, low_rank_done, blocks_over_x, grads_over_tok, grads_back]
    for k in range(ny - 1):
        ring_step(k)
        if side:
            side.pop(0)()
    for step in side:
        step()

    for j in range(2 * nq):
        qq, h = j // 2, j % 2
        for dx in range(nx):
            xx = (x + dx) % nx
            arrived(wq.at[xx, qq, h], fwd_r.at[xx, qq, h])
        out = dot(xg[0], wq[0, qq, h], 1, 0)
        for xx in range(1, nx):
            out = out + dot(xg[xx], wq[xx, qq, h], 1, 0)
        os_[j] = out.astype(BF16)
        zz = 4 * qq + 2 * c + h
        for cc in range(NC):
            send_or_keep(
                jnp.logical_and(z == zz, c == cc),
                os_.at[j, cc * hb:(cc + 1) * hb], orx.at[z], o_s.at[j, cc], o_r.at[z], dev(x, y, zz, cc),
            )
        for xx in range(nx):
            term = dot(gz[qq, h], wq[xx, qq, h], 1, 1)
            gxacc[xx] = term if j == 0 else gxacc[xx] + term
    for dx in range(nx):
        xx = (x + dx) % nx
        gxs[dx] = gxacc[xx].astype(BF16)
        for cc in range(NC):
            args = (gxs.at[dx, cc * hb:(cc + 1) * hb], gxr.at[x, c], q_s.at[dx, cc], q_r.at[x, c], dev(xx, y, z, cc))
            if dx:
                send(*args)
            else:
                send_or_keep(c == cc, *args)

    uv = uvt[...]
    out = dot(uv, ab[2], 1, 0)
    for zz in range(nz):
        arrived(orx.at[zz], o_r.at[zz])
        out = out + orx[zz].astype(F32)
    proj_ref[...] = out.astype(BF16)

    for dt in range(1, nt):
        tt = (tok + dt) % nt
        arrived(agb.at[tt], ag_r.at[tt])
    for tt in range(nt):
        r0 = tt * ra
        ref, r0 = (gradb_ref, r0) if r0 < rank else (grada_ref, r0 - rank)
        ref[r0:r0 + ra, 0:BLK] = agb[tt, 0:ra, :]
        ref[r0:r0 + ra, BLK:2 * BLK] = agb[tt, ra:2 * ra, :]
        gradblk_ref[tt * rb:(tt + 1) * rb, :] = agb[tt, 2 * ra:2 * ra + rb, :]

    out = dot(uv, ab[3], 1, 0)
    for xx in range(nx):
        for cc in range(NC):
            arrived(gxr.at[xx, cc], q_r.at[xx, cc])
            out = out + gxr[xx, cc].astype(F32)
    gradx_ref[...] = out.astype(BF16)

    for mine, copy in pending:
        if mine is None:
            copy.wait_send()
        else:
            pl.when(jnp.logical_not(mine))(copy.wait_send)


def make(dims):
    nx, ny, nz = dims
    nq, nt = ny // nx, ny * NC

    def on_device(activations, w_base, blk_vals, blk_index, blk_count, a_down, b_up, grad_out):
        hb, fb = activations.shape
        nsl, rank = blk_vals.shape[0], a_down.shape[1]
        scale = float(hb * nt) ** (-0.5)
        live = jnp.arange(nsl, dtype=jnp.int32) < blk_count[0]
        column = jnp.where(live, blk_index[:, 1], -1).astype(F32)
        table = jnp.zeros((8,), F32).at[0:nsl].set(column).at[4:4 + nsl].set(blk_index[:, 0].astype(F32))
        table = jnp.broadcast_to(table[:, None], (8, BLK))
        piece = 2 * (2 * rank // nt) + nsl * BLK // nt
        dma = pltpu.SemaphoreType.DMA
        vmem = pltpu.VMEM
        proj, gradx, grad_at, grad_b, blk = pl.pallas_call(
            functools.partial(kernel, dims, scale),
            out_shape=[
                jax.ShapeDtypeStruct((hb, fb), BF16),
                jax.ShapeDtypeStruct((hb, fb), BF16),
                jax.ShapeDtypeStruct((rank, fb), F32),
                jax.ShapeDtypeStruct((rank, fb), F32),
                jax.ShapeDtypeStruct((nsl * BLK, BLK), F32),
            ],
            in_specs=[pl.BlockSpec(memory_space=vmem)] * 7,
            out_specs=[pl.BlockSpec(memory_space=vmem)] * 5,
            scratch_shapes=[
                vmem((ny + 1, 2, fb, fb), BF16),
                vmem((nx, nq, 2, fb, fb), BF16),
                vmem((nx, NC * hb, fb), BF16),
                vmem((nq, 2, NC * hb, fb), BF16),
                vmem((nz, hb, fb), BF16),
                vmem((2 * nq, NC * hb, fb), BF16),
                vmem((nx, NC, hb, fb), BF16),
                vmem((nx, NC * hb, fb), BF16),
                vmem((nx, NC * hb, fb), F32),
                vmem((nx, hb, 2 * rank), BF16),
                vmem((nz, hb, 2 * rank), BF16),
                vmem((hb, 2 * rank), BF16),
                vmem((nx, 8, BLK), F32),
                vmem((nx, nsl * BLK, BLK), BF16),
                vmem((nx, nsl * BLK, BLK), BF16),
                vmem((nt, piece, BLK), F32),
                vmem((nt, piece, BLK), F32),
                vmem((nt, piece, BLK), F32),
                vmem((4, 2 * rank, fb), BF16),
                vmem((2 * rank, fb), F32),
                dma((2, ny)), dma((2, ny)),
                dma((ny + 1, 2)), dma((nx, nq, 2)),
                dma((nx, NC)), dma((nx, NC)),
                dma((nz,)), dma((nq, 2, NC)),
                dma((2 * nq, NC)), dma((nz,)),
                dma((nx, NC)), dma((nx, NC)),
                dma((nx,)), dma((nx,)),
                dma((nz,)), dma((nz,)),
                dma((nx,)), dma((nx,)),
                dma((nx,)), dma((nx,)),
                dma((nt,)), dma((nt,)),
                dma((nt,)), dma((nt,)),
            ],
            compiler_params=pltpu.CompilerParams(
                collective_id=0, has_side_effects=True, vmem_limit_bytes=40 * 1024 * 1024
            ),
        )(activations, w_base, blk_vals, table, a_down.T, b_up, grad_out)
        return proj, gradx, blk.reshape(nsl, BLK, BLK), grad_at.T, grad_b

    return on_device


def solution(mesh, dims=(4, 8, 8)):
    in_specs = (
        P("tok", "feat"),
        P("feat", "tok"),
        P("feat", None, None),
        P("feat", None),
        P("feat"),
        P("feat", None),
        P(None, "feat"),
        P("tok", "feat"),
    )
    out_specs = (
        P("tok", "feat"),
        P("tok", "feat"),
        P("feat", None, None),
        P("feat", None),
        P(None, "feat"),
    )
    return jax.shard_map(make(dims), mesh=mesh, in_specs=in_specs, out_specs=out_specs, check_vma=False)
```

```python
import functools

import jax
import jax.numpy as jnp
from jax import lax
from jax.experimental import pallas as pl
from jax.experimental.pallas import tpu as pltpu
from jax.sharding import PartitionSpec as P

MESH = pl.DeviceIdType.MESH
F32 = jnp.float32
BF16 = jnp.bfloat16
BLK = 128
NC = 2


def dot(a, b, ca, cb):
    return lax.dot_general(a, b, (((ca,), (cb,)), ((), ())), preferred_element_type=F32)


def kernel(
    dims, scale,
    x_in, w_in, blk_in, index_in, count_in, at_in, b_in, g_in,
    proj_ref, gradx_ref, grada_ref, gradb_ref, gradblk_ref,
    x_ref, w_ref, blk_ref, index_ref, count_ref, at_ref, b_ref, g_ref,
    wl, wq, xg, gz, orx, os_, gxr, gxs, gxacc, gss, gsr, up, ux, uz, ut, ug, idxg, bs, bx, br, tot, rss, rsr, agb, ab, gab,
    load_s, ring_s, ring_r, fwd_s, fwd_r, x_s, x_r, y_s, y_r, g_s, g_r, o_s, o_r, q_s, q_r, gs_s, gs_r,
    ux_s, ux_r, uz_s, uz_r, ug_s, ug_r, id_s, id_r, b_s, b_r, rs_s, rs_r, ag_s, ag_r,
):
    nx, ny, nz = dims
    nq = ny // nx
    nt = ny * NC
    half = ny // 2
    feat, tok = lax.axis_index("feat"), lax.axis_index("tok")
    x, z = feat // nz, feat % nz
    y, c = tok // NC, tok % NC
    zc = (z // 2) % 2
    zq, zh = z // (2 * NC), z % 2
    sib = 1 - c
    hb = x_ref.shape[0]
    pending = []

    def dev(xx, yy, zz, cc):
        return (xx * nz + zz, yy * NC + cc)

    def remote(src, dst, s_sem, r_sem, target):
        return pltpu.make_async_remote_copy(
            src_ref=src, dst_ref=dst, send_sem=s_sem, recv_sem=r_sem, device_id=target, device_id_type=MESH
        )

    def send(src, dst, s_sem, r_sem, target):
        copy = remote(src, dst, s_sem, r_sem, target)
        copy.start()
        pending.append((None, copy))

    def send_if(cond, src, dst, s_sem, r_sem, target):
        copy = remote(src, dst, s_sem, r_sem, target)
        pl.when(cond)(copy.start)
        pending.append((cond, copy))

    def send_or_keep(mine, src, dst, s_sem, r_sem, target):
        pl.when(mine)(pltpu.make_async_copy(src, dst, r_sem).start)
        send_if(jnp.logical_not(mine), src, dst, s_sem, r_sem, target)

    def arrived(dst, sem):
        pltpu.make_async_copy(dst, dst, sem).wait()

    barrier = pltpu.get_barrier_semaphore()
    greeted = 0
    for dz in range(1, nz):
        for cc in range(NC):
            pl.semaphore_signal(barrier, inc=1, device_id=dev(x, y, (z + dz) % nz, cc), device_id_type=MESH)
            greeted += 1
    for dt in range(1, nt):
        pl.semaphore_signal(barrier, inc=1, device_id=(feat, (tok + dt) % nt), device_id_type=MESH)
        greeted += 1
    for dx in range(1, nx):
        pl.semaphore_signal(barrier, inc=1, device_id=dev((x + dx) % nx, y, z, c), device_id_type=MESH)
        greeted += 1

    loads = []
    pairs = [
        (w_in, w_ref), (blk_in, blk_ref), (index_in, index_ref), (count_in, count_ref),
        (x_in, x_ref), (at_in, at_ref), (g_in, g_ref), (b_in, b_ref),
    ]
    for i, (src, dst) in enumerate(pairs):
        copy = pltpu.make_async_copy(src, dst, load_s.at[i])
        copy.start()
        loads.append(copy)
    for copy in loads[:4]:
        copy.wait()

    nsl = blk_ref.shape[0]
    for j in range(nsl):
        col = jnp.where(count_ref[...] > j, index_ref[1:2, j:j + 1], -1).astype(F32)
        idxg[x, j:j + 1, :] = jnp.broadcast_to(col, (1, BLK))
        idxg[x, 4 + j:5 + j, :] = jnp.broadcast_to(index_ref[0:1, j:j + 1].astype(F32), (1, BLK))
    for h in range(2):
        for rr in range(2):
            for hh in range(2):
                r0, c0 = rr * BLK, h * 2 * BLK + hh * BLK
                piece = w_ref[r0:r0 + BLK, c0:c0 + BLK].astype(F32)
                column = (tok * 4 + h * 2 + hh).astype(F32)
                for j in range(nsl):
                    hit = jnp.where(idxg[x, j:j + 1, :] == column, 1.0, 0.0) * jnp.where(
                        idxg[x, 4 + j:5 + j, :] == float(rr), 1.0, 0.0
                    )
                    piece = piece + hit * blk_ref[j].astype(F32)
                wl[0, h, r0:r0 + BLK, hh * BLK:(hh + 1) * BLK] = piece.astype(BF16)

    for copy in loads[4:]:
        copy.wait()
    rank = at_ref.shape[0]
    ab[...] = jnp.zeros_like(ab)
    ab[0, 0:rank, :] = at_ref[...]
    ab[1, rank:2 * rank, :] = b_ref[...]
    ab[2, 0:rank, :] = b_ref[...]
    ab[3, rank:2 * rank, :] = at_ref[...]
    part = (dot(x_ref[...], ab[0], 1, 1) + dot(g_ref[...], ab[1], 1, 1)).astype(BF16)
    ur = hb // nx
    for xx in range(nx):
        up[xx] = part[xx * ur:(xx + 1) * ur]

    pl.semaphore_wait(barrier, greeted)

    last = ny - 2

    def ring_slot(direction, k):
        d, sub = k // 2 + 1, (k + direction) % 2
        return (d if direction == 0 else half + d), d, sub

    def ring_send(direction, k):
        if k > last:
            return
        if k < 2:
            src = wl.at[0, (k + direction) % 2]
        else:
            slot, _, sub = ring_slot(direction, k - 2)
            src = wl.at[slot, sub]
        slot, _, sub = ring_slot(direction, k)
        to = (y + 1) % ny if direction == 0 else (y + ny - 1) % ny
        send(src, wl.at[slot, sub], ring_s.at[direction, k], ring_r.at[direction, k], dev(x, to, z, c))

    def hand_on(slot, sub, yy):
        xx, qq = yy // nq, yy % nq
        send_or_keep(
            x == xx, wl.at[slot, sub], wq.at[x, qq, sub], fwd_s.at[slot, sub], fwd_r.at[x, qq, sub], dev(xx, y, z, c)
        )

    def row_of(direction, d):
        return (y + ny - d) % ny if direction == 0 else (y + d) % ny

    def ring_step(k):
        for direction in range(2):
            slot, d, sub = ring_slot(direction, k)
            arrived(wl.at[slot, sub], ring_r.at[direction, k])
            ring_send(direction, k + 2)
            hand_on(slot, sub, row_of(direction, d))

    mine_rows = pl.ds(pl.multiple_of(c * hb, hb), hb)
    for k in range(2):
        for direction in range(2):
            ring_send(direction, k)
    for dx in range(1, nx):
        xx = (x + dx) % nx
        send(up.at[xx], ux.at[x], ux_s.at[dx], ux_r.at[x], dev(xx, y, z, c))
        send(idxg.at[x], idxg.at[x], id_s.at[dx], id_r.at[x], dev(xx, y, z, c))
    for dx in range(1, nx):
        send(x_ref, xg.at[x, mine_rows], x_s.at[dx], x_r.at[x], dev((x + dx) % nx, y, z, c))
    pltpu.make_async_copy(x_ref, xg.at[x, mine_rows], x_r.at[x]).start()
    for h in range(2):
        hand_on(0, h, y)

    def low_rank_over_z():
        total = up[x].astype(F32)
        for dx in range(1, nx):
            xx = (x + dx) % nx
            arrived(ux.at[xx], ux_r.at[xx])
            total = total + ux[xx].astype(F32)
        uz[z] = total.astype(BF16)
        for dz in range(1, nz):
            send(uz.at[z], uz.at[z], uz_s.at[dz], uz_r.at[z], dev(x, y, (z + dz) % nz, c))

    def cotangent_over_z():
        for dz in range(nz):
            args = (g_ref, gz.at[zq, zh, mine_rows], g_s.at[dz], g_r.at[zq, zh, c], dev(x, y, (z + dz) % nz, zc))
            if dz:
                send(*args)
            else:
                send_or_keep(c == zc, *args)

    def activations_on_chip():
        for dx in range(nx):
            xx = (x + dx) % nx
            arrived(xg.at[xx, mine_rows], x_r.at[xx])
            send(xg.at[xx, mine_rows], xg.at[xx, mine_rows], y_s.at[xx], y_r.at[xx], dev(x, y, z, sib))

    def low_rank_over_x():
        total = uz[z].astype(F32)
        for dz in range(1, nz):
            zz = (z + dz) % nz
            arrived(uz.at[zz], uz_r.at[zz])
            total = total + uz[zz].astype(F32)
        ut[x] = total.astype(BF16)
        for dx in range(1, nx):
            send(ut.at[x], ut.at[x], ug_s.at[dx], ug_r.at[x], dev((x + dx) % nx, y, z, c))

    def low_rank_done():
        for dx in range(1, nx):
            xx = (x + dx) % nx
            arrived(ut.at[xx], ug_r.at[xx])
        for xx in range(nx):
            ug[xx * ur:(xx + 1) * ur, :] = ut[xx]
        uv = ug[...]
        gab[0:rank] = dot(uv, g_ref[...], 0, 0)[0:rank]
        gab[rank:2 * rank] = dot(uv, x_ref[...], 0, 0)[rank:2 * rank]

    def blocks_over_x():
        other_rows = pl.ds(pl.multiple_of(sib * hb, hb), hb)
        for dx in range(nx):
            xx = (x + dx) % nx
            if dx:
                arrived(idxg.at[xx], id_r.at[xx])
            arrived(xg.at[xx, other_rows], y_r.at[xx])
        for qq in range(nq):
            for h in range(2):
                for cc in range(NC):
                    arrived(gz.at[qq, h, cc * hb:(cc + 1) * hb], g_r.at[qq, h, cc])
        for dx in range(nx):
            xx = (x + dx) % nx
            for j in range(nsl):
                col, row = idxg[xx, j:j + 1, :], idxg[xx, 4 + j:5 + j, :]
                picked = jnp.zeros((NC * hb, BLK), BF16)
                for qq in range(nq):
                    for h in range(2):
                        base = (2 * (x * nz + 4 * qq + 2 * c + h)).astype(F32)
                        for hh in range(2):
                            hit = jnp.where(col == base + float(hh), 1.0, 0.0).astype(BF16)
                            picked = picked + gz[qq, h, :, hh * BLK:(hh + 1) * BLK] * hit
                top = jnp.where(row == 0.0, 1.0, 0.0).astype(BF16)
                low = jnp.where(row == 1.0, 1.0, 0.0).astype(BF16)
                xs = xg[xx, :, 0:BLK] * top + xg[xx, :, BLK:2 * BLK] * low
                bs[dx, j * BLK:(j + 1) * BLK, :] = dot(xs, picked, 0, 0)

    ra, rb = 2 * rank // nt, nsl * BLK // nt

    def grads_over_tok():
        for tt in range(nt):
            rows = gab[tt * ra:(tt + 1) * ra]
            rss[tt, 0:2 * ra, :] = jnp.concatenate([rows[:, 0:BLK], rows[:, BLK:2 * BLK]], axis=0).astype(BF16)
            for dx in range(nx):
                r0 = 2 * ra + dx * rb
                rss[tt, r0:r0 + rb, :] = bs[dx, tt * rb:(tt + 1) * rb, :].astype(BF16)
        rsr[tok] = rss[tok]
        for dt in range(1, nt):
            tt = (tok + dt) % nt
            send(rss.at[tt], rsr.at[tok], rs_s.at[dt], rs_r.at[tok], (feat, tt))

    def blocks_home():
        total = rsr[tok].astype(F32)
        for dt in range(1, nt):
            tt = (tok + dt) % nt
            arrived(rsr.at[tt], rs_r.at[tt])
            total = total + rsr[tt].astype(F32)
        part = total[0:2 * ra]
        tot[0:2 * ra, :] = part
        for dx in range(nx):
            r0 = 2 * ra + dx * rb
            bx[dx] = total[r0:r0 + rb].astype(BF16)
            if dx:
                send(bx.at[dx], br.at[x], b_s.at[dx], b_r.at[x], dev((x + dx) % nx, y, z, c))
        tot[2 * ra:2 * ra + rb, :] = total[2 * ra:2 * ra + rb]

    def grads_back():
        total = tot[2 * ra:2 * ra + rb, :]
        for dx in range(1, nx):
            xx = (x + dx) % nx
            arrived(br.at[xx], b_r.at[xx])
            total = total + br[xx].astype(F32)
        tot[2 * ra:2 * ra + rb, :] = total
        agb[tok] = (tot[...] * scale).astype(BF16)
        for dt in range(1, nt):
            send(agb.at[tok], agb.at[tok], ag_s.at[dt], ag_r.at[tok], (feat, (tok + dt) % nt))

    def chunk(step):
        h = (step + z) % 2
        near = (y // nq - x) % nx < nx // 2
        qq = jnp.where(near, nq - 1 - step // 2, step // 2)
        for dx in range(nx):
            xx = (x + dx) % nx
            arrived(wq.at[xx, qq, h], fwd_r.at[xx, qq, h])
        out = dot(xg[0], wq[0, qq, h], 1, 0)
        for xx in range(1, nx):
            out = out + dot(xg[xx], wq[xx, qq, h], 1, 0)
        os_[step] = out.astype(BF16)
        zz = 4 * qq + 2 * c + h
        for cc in range(NC):
            send_or_keep(
                jnp.logical_and(z == zz, c == cc),
                os_.at[step, cc * hb:(cc + 1) * hb], orx.at[z], o_s.at[step, cc], o_r.at[z], dev(x, y, zz, cc),
            )
        for xx in range(nx):
            term = dot(gz[qq, h], wq[xx, qq, h], 1, 1)
            gxacc[xx] = term if step == 0 else gxacc[xx] + term

    def inputs_on_chip():
        other_rows = pl.ds(pl.multiple_of(sib * hb, hb), hb)
        gss[...] = gxacc[:, other_rows, :].astype(BF16)
        send(gss, gsr, gs_s.at[0], gs_r.at[0], dev(x, y, z, sib))

    def inputs_over_x():
        arrived(gsr, gs_r.at[0])
        for dx in range(nx):
            xx = (x + dx) % nx
            gxs[dx] = (gxacc[xx, mine_rows, :] + gsr[xx].astype(F32)).astype(BF16)
            if dx:
                send(gxs.at[dx], gxr.at[x], q_s.at[dx], q_r.at[x], dev(xx, y, z, c))

    low_rank_over_z()
    cotangent_over_z()
    after = {1: [activations_on_chip], 2: [low_rank_over_x]}
    for k in range(ny - 1):
        ring_step(k)
        for side in after.pop(k, []):
            side()
    for k in sorted(after):
        for side in after[k]:
            side()
    blocks_over_x()
    low_rank_done()
    grads_over_tok()
    for step in range(2 * nq):
        chunk(step)
        if step == nq - 1:
            blocks_home()
    inputs_on_chip()
    grads_back()
    inputs_over_x()

    uv = ug[...]
    out = dot(uv, ab[2], 1, 0)
    for zz in range(nz):
        arrived(orx.at[zz], o_r.at[zz])
        out = out + orx[zz].astype(F32)
    proj_ref[...] = out.astype(BF16)

    out = dot(uv, ab[3], 1, 0) + gxs[0].astype(F32)
    for dx in range(1, nx):
        xx = (x + dx) % nx
        arrived(gxr.at[xx], q_r.at[xx])
        out = out + gxr[xx].astype(F32)
    gradx_ref[...] = out.astype(BF16)

    for dt in range(1, nt):
        tt = (tok + dt) % nt
        arrived(agb.at[tt], ag_r.at[tt])
    for tt in range(nt):
        r0 = tt * ra
        ref, r0 = (gradb_ref, r0) if r0 < rank else (grada_ref, r0 - rank)
        back = agb[tt].astype(F32)
        ref[r0:r0 + ra, 0:BLK] = back[0:ra]
        ref[r0:r0 + ra, BLK:2 * BLK] = back[ra:2 * ra]
        gradblk_ref[tt * rb:(tt + 1) * rb, :] = back[2 * ra:2 * ra + rb]

    for cond, copy in pending:
        if cond is None:
            copy.wait_send()
        else:
            pl.when(cond)(copy.wait_send)


def write_out(*refs):
    n = 5
    load, store = refs[3 * n], refs[3 * n + 1]
    ins = [pltpu.make_async_copy(refs[i], refs[2 * n + i], load.at[i]) for i in range(n)]
    outs = [pltpu.make_async_copy(refs[2 * n + i], refs[n + i], store.at[i]) for i in range(n)]
    for copy in ins:
        copy.start()
    for i in range(n):
        ins[i].wait()
        outs[i].start()
    for copy in outs:
        copy.wait()


def make(dims):
    nx, ny, nz = dims
    nq, nt = ny // nx, ny * NC

    def on_device(activations, w_base, blk_vals, blk_index, blk_count, a_down, b_up, grad_out):
        hb, fb = activations.shape
        nsl, rank = blk_vals.shape[0], a_down.shape[1]
        scale = float(hb * nt) ** (-0.5)
        ra, rb = 2 * rank // nt, nsl * BLK // nt
        dma = pltpu.SemaphoreType.DMA
        vmem = pltpu.VMEM
        shapes = [
            jax.ShapeDtypeStruct((hb, fb), BF16),
            jax.ShapeDtypeStruct((hb, fb), BF16),
            jax.ShapeDtypeStruct((rank, fb), F32),
            jax.ShapeDtypeStruct((rank, fb), F32),
            jax.ShapeDtypeStruct((nsl * BLK, BLK), F32),
        ]
        results = pl.pallas_call(
            functools.partial(kernel, dims, scale),
            out_shape=shapes,
            in_specs=[pl.BlockSpec(memory_space=pltpu.HBM)] * 8,
            out_specs=[pl.BlockSpec(memory_space=vmem)] * 5,
            scratch_shapes=[
                vmem((hb, fb), BF16), vmem((fb, 2 * fb), BF16), vmem((nsl, BLK, BLK), BF16), vmem((2, nsl), jnp.int32),
                vmem((1, 1), jnp.int32), vmem((rank, fb), BF16), vmem((rank, fb), BF16), vmem((hb, fb), BF16),
                vmem((ny + 1, 2, fb, fb), BF16),
                vmem((nx, nq, 2, fb, fb), BF16),
                vmem((nx, NC * hb, fb), BF16),
                vmem((nq, 2, NC * hb, fb), BF16),
                vmem((nz, hb, fb), BF16),
                vmem((2 * nq, NC * hb, fb), BF16),
                vmem((nx, hb, fb), BF16),
                vmem((nx, hb, fb), BF16),
                vmem((nx, NC * hb, fb), F32),
                vmem((nx, hb, fb), BF16),
                vmem((nx, hb, fb), BF16),
                vmem((nx, hb // nx, 2 * rank), BF16),
                vmem((nx, hb // nx, 2 * rank), BF16),
                vmem((nz, hb // nx, 2 * rank), BF16),
                vmem((nx, hb // nx, 2 * rank), BF16),
                vmem((hb, 2 * rank), BF16),
                vmem((nx, 8, BLK), F32),
                vmem((nx, nsl * BLK, BLK), F32),
                vmem((nx, rb, BLK), BF16),
                vmem((nx, rb, BLK), BF16),
                vmem((2 * ra + rb, BLK), F32),
                vmem((nt, 2 * ra + nx * rb, BLK), BF16),
                vmem((nt, 2 * ra + nx * rb, BLK), BF16),
                vmem((nt, 2 * ra + rb, BLK), BF16),
                vmem((4, 2 * rank, fb), BF16),
                vmem((2 * rank, fb), F32),
                dma((8,)),
                dma((2, ny)), dma((2, ny)),
                dma((ny + 1, 2)), dma((nx, nq, 2)),
                dma((nx,)), dma((nx,)),
                dma((nx,)), dma((nx,)),
                dma((nz,)), dma((nq, 2, NC)),
                dma((2 * nq, NC)), dma((nz,)),
                dma((nx,)), dma((nx,)),
                dma((1,)), dma((1,)),
                dma((nx,)), dma((nx,)),
                dma((nz,)), dma((nz,)),
                dma((nx,)), dma((nx,)),
                dma((nx,)), dma((nx,)),
                dma((nx,)), dma((nx,)),
                dma((nt,)), dma((nt,)),
                dma((nt,)), dma((nt,)),
            ],
            compiler_params=pltpu.CompilerParams(
                collective_id=0, has_side_effects=True, vmem_limit_bytes=63 * 1024 * 1024
            ),
        )(activations, w_base, blk_vals, blk_index.T, blk_count.reshape(1, 1), a_down.T, b_up, grad_out)
        proj, gradx, grad_at, grad_b, blk = pl.pallas_call(
            write_out,
            out_shape=shapes,
            in_specs=[pl.BlockSpec(memory_space=pltpu.HBM)] * 5,
            out_specs=[pl.BlockSpec(memory_space=pltpu.HBM)] * 5,
            scratch_shapes=[vmem(s.shape, s.dtype) for s in shapes] + [dma((5,)), dma((5,))],
            compiler_params=pltpu.CompilerParams(vmem_limit_bytes=63 * 1024 * 1024),
        )(*results)
        return proj, gradx, blk.reshape(nsl, BLK, BLK), grad_at.T, grad_b

    return on_device


def solution(mesh, dims=(4, 8, 8)):
    in_specs = (
        P("tok", "feat"),
        P("feat", "tok"),
        P("feat", None, None),
        P("feat", None),
        P("feat"),
        P("feat", None),
        P(None, "feat"),
        P("tok", "feat"),
    )
    out_specs = (
        P("tok", "feat"),
        P("tok", "feat"),
        P("feat", None, None),
        P("feat", None),
        P(None, "feat"),
    )
    return jax.shard_map(make(dims), mesh=mesh, in_specs=in_specs, out_specs=out_specs, check_vma=False)
```

```python
import functools

import jax
import jax.numpy as jnp
from jax import lax
from jax.experimental import pallas as pl
from jax.experimental.pallas import tpu as pltpu
from jax.sharding import PartitionSpec as P

MESH = pl.DeviceIdType.MESH
F32 = jnp.float32
BF16 = jnp.bfloat16
BLK = 128
NC = 2


def dot(a, b, ca, cb):
    return lax.dot_general(a, b, (((ca,), (cb,)), ((), ())), preferred_element_type=F32)


def kernel(
    dims, scale,
    x_in, w_in, blk_in, index_in, count_in, at_in, b_in, g_in,
    proj_ref, gradx_ref, grada_ref, gradb_ref, gradblk_ref,
    x_ref, w_ref, blk_ref, index_ref, count_ref, at_ref, b_ref, g_ref,
    wl, wq, xg, gz, orx, os_, gxr, gxs, gxacc, gss, gsr, up, ux, uz, ut, ug, idxg, bs, bss, bsr, gas, gar, bx, br, tot, rss, rsr, agb, ab, gab,
    load_s, ring_s, ring_r, fwd_s, fwd_r, far_s, x_s, x_r, y_s, y_r, g_s, g_r, o_s, o_r, q_s, q_r, gs_s, gs_r,
    ux_s, ux_r, uz_s, uz_r, ug_s, ug_r, id_s, id_r, bc_s, bc_r, b_s, b_r, rs_s, rs_r, ag_s, ag_r,
):
    nx, ny, nz = dims
    nq = ny // nx
    nt = ny * NC
    half = ny // 2
    feat, tok = lax.axis_index("feat"), lax.axis_index("tok")
    x, z = feat // nz, feat % nz
    y, c = tok // NC, tok % NC
    zc = (z // 2) % 2
    zq, zh = z // (2 * NC), z % 2
    sib = 1 - c
    hb = x_ref.shape[0]
    pending = []

    def dev(xx, yy, zz, cc):
        return (xx * nz + zz, yy * NC + cc)

    def remote(src, dst, s_sem, r_sem, target):
        return pltpu.make_async_remote_copy(
            src_ref=src, dst_ref=dst, send_sem=s_sem, recv_sem=r_sem, device_id=target, device_id_type=MESH
        )

    def send(src, dst, s_sem, r_sem, target):
        copy = remote(src, dst, s_sem, r_sem, target)
        copy.start()
        pending.append((None, copy))

    def send_if(cond, src, dst, s_sem, r_sem, target):
        copy = remote(src, dst, s_sem, r_sem, target)
        pl.when(cond)(copy.start)
        pending.append((cond, copy))

    def send_or_keep(mine, src, dst, s_sem, r_sem, target):
        pl.when(mine)(pltpu.make_async_copy(src, dst, r_sem).start)
        send_if(jnp.logical_not(mine), src, dst, s_sem, r_sem, target)

    def arrived(dst, sem):
        pltpu.make_async_copy(dst, dst, sem).wait()

    barrier = pltpu.get_barrier_semaphore()
    greeted = 0
    for dz in range(1, nz):
        for cc in range(NC):
            pl.semaphore_signal(barrier, inc=1, device_id=dev(x, y, (z + dz) % nz, cc), device_id_type=MESH)
            greeted += 1
    for dt in range(1, nt):
        pl.semaphore_signal(barrier, inc=1, device_id=(feat, (tok + dt) % nt), device_id_type=MESH)
        greeted += 1
    for dx in range(1, nx):
        for cc in range(NC):
            pl.semaphore_signal(barrier, inc=1, device_id=dev((x + dx) % nx, y, z, cc), device_id_type=MESH)
            greeted += 1

    loads = []
    pairs = [
        (w_in, w_ref), (blk_in, blk_ref), (index_in, index_ref), (count_in, count_ref),
        (x_in, x_ref), (at_in, at_ref), (g_in, g_ref), (b_in, b_ref),
    ]
    for i, (src, dst) in enumerate(pairs):
        copy = pltpu.make_async_copy(src, dst, load_s.at[i])
        copy.start()
        loads.append(copy)
    for copy in loads[:4]:
        copy.wait()

    nsl = blk_ref.shape[0]
    for j in range(nsl):
        col = jnp.where(count_ref[...] > j, index_ref[1:2, j:j + 1], -1).astype(F32)
        idxg[x, j:j + 1, :] = jnp.broadcast_to(col, (1, BLK))
        idxg[x, 4 + j:5 + j, :] = jnp.broadcast_to(index_ref[0:1, j:j + 1].astype(F32), (1, BLK))
    for h in range(2):
        for rr in range(2):
            for hh in range(2):
                r0, c0 = rr * BLK, h * 2 * BLK + hh * BLK
                piece = w_ref[r0:r0 + BLK, c0:c0 + BLK].astype(F32)
                column = (tok * 4 + h * 2 + hh).astype(F32)
                for j in range(nsl):
                    hit = jnp.where(idxg[x, j:j + 1, :] == column, 1.0, 0.0) * jnp.where(
                        idxg[x, 4 + j:5 + j, :] == float(rr), 1.0, 0.0
                    )
                    piece = piece + hit * blk_ref[j].astype(F32)
                wl[0, h, r0:r0 + BLK, hh * BLK:(hh + 1) * BLK] = piece.astype(BF16)

    for copy in loads[4:]:
        copy.wait()
    rank = at_ref.shape[0]
    ab[...] = jnp.zeros_like(ab)
    ab[0, 0:rank, :] = at_ref[...]
    ab[1, rank:2 * rank, :] = b_ref[...]
    ab[2, 0:rank, :] = b_ref[...]
    ab[3, rank:2 * rank, :] = at_ref[...]
    part = (dot(x_ref[...], ab[0], 1, 1) + dot(g_ref[...], ab[1], 1, 1)).astype(BF16)
    ur = hb // nx
    for xx in range(nx):
        up[xx] = part[xx * ur:(xx + 1) * ur]

    pl.semaphore_wait(barrier, greeted)

    last = ny - 2

    def ring_slot(direction, k):
        d, sub = k // 2 + 1, (k + direction) % 2
        return (d if direction == 0 else half + d), d, sub

    def ring_send(direction, k):
        if k > last:
            return
        if k < 2:
            src = wl.at[0, (k + direction) % 2]
        else:
            slot, _, sub = ring_slot(direction, k - 2)
            src = wl.at[slot, sub]
        slot, _, sub = ring_slot(direction, k)
        to = (y + 1) % ny if direction == 0 else (y + ny - 1) % ny
        send(src, wl.at[slot, sub], ring_s.at[direction, k], ring_r.at[direction, k], dev(x, to, z, c))

    home = x == y // nq

    def hand_on(slot, sub, yy):
        xx, qq = yy // nq, yy % nq
        if far(slot, sub):
            pl.when(x == xx)(pltpu.make_async_copy(wl.at[slot, sub], wq.at[x, qq, sub], fwd_r.at[x, qq, sub]).start)
            return
        send_or_keep(
            x == xx, wl.at[slot, sub], wq.at[x, qq, sub], fwd_s.at[slot, sub], fwd_r.at[x, qq, sub], dev(xx, y, z, c)
        )

    def far(slot, sub):
        return nx == 4 and slot == 2 * half and sub == 1

    def to_far_row():
        qq = y % nq
        for dx in range(1, nx):
            xx = (x + dx) % nx
            piece = wq.at[xx, qq, 1]
            pl.when(home)(pltpu.make_async_copy(piece, piece, fwd_r.at[xx, qq, 1]).wait)
            send_if(home, piece, piece, far_s.at[dx], fwd_r.at[xx, qq, 1], dev(x, (y + half) % ny, z, c))

    def row_of(direction, d):
        return (y + ny - d) % ny if direction == 0 else (y + d) % ny

    def ring_step(k):
        for direction in range(2):
            slot, d, sub = ring_slot(direction, k)
            arrived(wl.at[slot, sub], ring_r.at[direction, k])
            ring_send(direction, k + 2)
            if k != ny - 3:
                hand_on(slot, sub, row_of(direction, d))
        if k == ny - 2 and k:
            for direction in range(2):
                slot, d, sub = ring_slot(direction, k - 1)
                hand_on(slot, sub, row_of(direction, d))

    mine_rows = pl.ds(pl.multiple_of(c * hb, hb), hb)
    for k in range(2):
        for direction in range(2):
            ring_send(direction, k)
    for dx in range(1, nx):
        xx = (x + dx) % nx
        send(up.at[xx], ux.at[x], ux_s.at[dx], ux_r.at[x], dev(xx, y, z, c))
        send(idxg.at[x], idxg.at[x], id_s.at[dx], id_r.at[x], dev(xx, y, z, c))
    for dx in range(1, nx):
        send(x_ref, xg.at[x, mine_rows], x_s.at[dx], x_r.at[x], dev((x + dx) % nx, y, z, c))
    pltpu.make_async_copy(x_ref, xg.at[x, mine_rows], x_r.at[x]).start()
    for h in range(2):
        hand_on(0, h, y)

    def low_rank_over_z():
        total = up[x].astype(F32)
        for dx in range(1, nx):
            xx = (x + dx) % nx
            arrived(ux.at[xx], ux_r.at[xx])
            total = total + ux[xx].astype(F32)
        uz[z] = total.astype(BF16)
        for dz in range(1, nz):
            send(uz.at[z], uz.at[z], uz_s.at[dz], uz_r.at[z], dev(x, y, (z + dz) % nz, c))

    def cotangent_over_z(distances):
        for dz in distances:
            args = (g_ref, gz.at[zq, zh, mine_rows], g_s.at[dz], g_r.at[zq, zh, c], dev(x, y, (z + dz) % nz, zc))
            if dz:
                send(*args)
            else:
                send_or_keep(c == zc, *args)

    def activations_on_chip():
        for dx in range(nx):
            xx = (x + dx) % nx
            arrived(xg.at[xx, mine_rows], x_r.at[xx])
            send(xg.at[xx, mine_rows], xg.at[xx, mine_rows], y_s.at[xx], y_r.at[xx], dev(x, y, z, sib))

    def low_rank_over_x():
        total = uz[z].astype(F32)
        for dz in range(1, nz):
            zz = (z + dz) % nz
            arrived(uz.at[zz], uz_r.at[zz])
            total = total + uz[zz].astype(F32)
        ut[x] = total.astype(BF16)
        for dx in range(1, nx):
            send(ut.at[x], ut.at[x], ug_s.at[dx], ug_r.at[x], dev((x + dx) % nx, y, z, c))

    def low_rank_done():
        for dx in range(1, nx):
            xx = (x + dx) % nx
            arrived(ut.at[xx], ug_r.at[xx])
        for xx in range(nx):
            ug[xx * ur:(xx + 1) * ur, :] = ut[xx]
        uv = ug[...]
        gab[0:rank] = dot(uv, g_ref[...], 0, 0)[0:rank]
        gab[rank:2 * rank] = dot(uv, x_ref[...], 0, 0)[rank:2 * rank]

    def blocks_over_x():
        other_rows = pl.ds(pl.multiple_of(sib * hb, hb), hb)
        for dx in range(nx):
            xx = (x + dx) % nx
            if dx:
                arrived(idxg.at[xx], id_r.at[xx])
            arrived(xg.at[xx, other_rows], y_r.at[xx])
        for qq in range(nq):
            for h in range(2):
                for cc in range(NC):
                    arrived(gz.at[qq, h, cc * hb:(cc + 1) * hb], g_r.at[qq, h, cc])
        for dx in range(nx):
            xx = (x + dx) % nx
            for j in range(nsl):
                col, row = idxg[xx, j:j + 1, :], idxg[xx, 4 + j:5 + j, :]
                picked = jnp.zeros((NC * hb, BLK), BF16)
                for qq in range(nq):
                    for h in range(2):
                        base = (2 * (x * nz + 4 * qq + 2 * c + h)).astype(F32)
                        for hh in range(2):
                            hit = jnp.where(col == base + float(hh), 1.0, 0.0).astype(BF16)
                            picked = picked + gz[qq, h, :, hh * BLK:(hh + 1) * BLK] * hit
                top = jnp.where(row == 0.0, 1.0, 0.0).astype(BF16)
                low = jnp.where(row == 1.0, 1.0, 0.0).astype(BF16)
                xs = xg[xx, :, 0:BLK] * top + xg[xx, :, BLK:2 * BLK] * low
                bs[dx, j * BLK:(j + 1) * BLK, :] = dot(xs, picked, 0, 0)

    ra, rb = rank // ny, nsl * BLK // nt
    hx = nx // NC

    def blocks_on_chip():
        for i in range(hx):
            bss[i] = bs[sib * hx + i].astype(BF16)
        send(bss, bsr, bc_s.at[0], bc_r.at[0], dev(x, y, z, sib))

    def low_rank_on_chip():
        gas[...] = gab[pl.ds(pl.multiple_of(sib * rank, rank), rank)].astype(BF16)
        send(gas, gar, bc_s.at[1], bc_r.at[1], dev(x, y, z, sib))

    def grads_over_tok():
        arrived(bsr, bc_r.at[0])
        for i in range(hx):
            rows = bs[c * hx + i] + bsr[i].astype(F32)
            for yy in range(ny):
                r0 = 2 * ra + i * NC * rb
                rss[yy, r0:r0 + NC * rb, :] = rows[yy * NC * rb:(yy + 1) * NC * rb].astype(BF16)
        arrived(gar, bc_r.at[1])
        sums = gab[pl.ds(pl.multiple_of(c * rank, rank), rank)] + gar[...].astype(F32)
        for yy in range(ny):
            rows = sums[yy * ra:(yy + 1) * ra]
            rss[yy, 0:2 * ra, :] = jnp.concatenate([rows[:, 0:BLK], rows[:, BLK:2 * BLK]], axis=0).astype(BF16)
        rsr[y] = rss[y]
        for dy in range(1, ny):
            yy = (y + dy) % ny
            send(rss.at[yy], rsr.at[y], rs_s.at[dy], rs_r.at[y], dev(x, yy, z, c))

    def blocks_home():
        total = rsr[y].astype(F32)
        for dy in range(1, ny):
            yy = (y + dy) % ny
            arrived(rsr.at[yy], rs_r.at[yy])
            total = total + rsr[yy].astype(F32)
        tot[0:2 * ra, :] = total[0:2 * ra]
        for i in range(hx):
            xx = (x + c * hx + i) % nx
            for cc in range(NC):
                r0 = 2 * ra + (i * NC + cc) * rb
                bx[i, cc] = total[r0:r0 + rb].astype(BF16)
                args = (bx.at[i, cc], br.at[x], b_s.at[i, cc], b_r.at[x], dev(xx, y, z, cc))
                if i == 0 and cc == 0:
                    send_or_keep(c == 0, *args)
                else:
                    send(*args)

    def grads_back():
        total = jnp.zeros((rb, BLK), F32)
        for xx in range(nx):
            arrived(br.at[xx], b_r.at[xx])
            total = total + br[xx].astype(F32)
        tot[2 * ra:2 * ra + rb, :] = total
        agb[tok] = (tot[...] * scale).astype(BF16)
        for dt in range(1, nt):
            send(agb.at[tok], agb.at[tok], ag_s.at[dt], ag_r.at[tok], (feat, (tok + dt) % nt))

    def chunk(step):
        if nq == 1:
            qq, h = 0, step
        elif step % 2:
            qq, h = y % 2, step // 2
        else:
            qq, h = 1 - y % 2, (y + step // 2) % 2
        early = jnp.logical_and(home, jnp.logical_and(qq == y % nq, h == 1)) if nx == 4 else None
        for dx in range(nx):
            xx = (x + dx) % nx
            piece = wq.at[xx, qq, h]
            if dx and nx == 4:
                pl.when(jnp.logical_not(early))(pltpu.make_async_copy(piece, piece, fwd_r.at[xx, qq, h]).wait)
            else:
                arrived(piece, fwd_r.at[xx, qq, h])
        out = dot(xg[0], wq[0, qq, h], 1, 0)
        for xx in range(1, nx):
            out = out + dot(xg[xx], wq[xx, qq, h], 1, 0)
        os_[step] = out.astype(BF16)
        zz = 4 * qq + 2 * c + h
        for cc in range(NC):
            send_or_keep(
                jnp.logical_and(z == zz, c == cc),
                os_.at[step, cc * hb:(cc + 1) * hb], orx.at[z], o_s.at[step, cc], o_r.at[z], dev(x, y, zz, cc),
            )
        for xx in range(nx):
            term = dot(gz[qq, h], wq[xx, qq, h], 1, 1)
            gxacc[xx] = term if step == 0 else gxacc[xx] + term

    def inputs_on_chip():
        other_rows = pl.ds(pl.multiple_of(sib * hb, hb), hb)
        gss[...] = gxacc[:, other_rows, :].astype(BF16)
        send(gss, gsr, gs_s.at[0], gs_r.at[0], dev(x, y, z, sib))

    def inputs_over_x():
        arrived(gsr, gs_r.at[0])
        for dx in range(nx):
            xx = (x + dx) % nx
            gxs[dx] = (gxacc[xx, mine_rows, :] + gsr[xx].astype(F32)).astype(BF16)
            if dx:
                send(gxs.at[dx], gxr.at[x], q_s.at[dx], q_r.at[x], dev(xx, y, z, c))

    around = sorted(range(nz), key=lambda dz: -min(dz, nz - dz))
    cotangent_over_z(around[:3])
    low_rank_over_z()
    cotangent_over_z(around[3:])
    after = {1: [activations_on_chip], 2: [low_rank_over_x], ny - 4: [to_far_row] if nx == 4 else []}
    for k in range(ny - 1):
        ring_step(k)
        for side in after.pop(k, []):
            side()
    for k in sorted(after):
        for side in after[k]:
            side()
    blocks_over_x()
    blocks_on_chip()
    low_rank_done()
    low_rank_on_chip()
    grads_over_tok()
    for step in range(2 * nq):
        chunk(step)
        if step == nq - 1:
            blocks_home()
    inputs_on_chip()
    grads_back()
    inputs_over_x()

    uv = ug[...]
    out = dot(uv, ab[2], 1, 0)
    for zz in range(nz):
        arrived(orx.at[zz], o_r.at[zz])
        out = out + orx[zz].astype(F32)
    proj_ref[...] = out.astype(BF16)

    out = dot(uv, ab[3], 1, 0) + gxs[0].astype(F32)
    for dx in range(1, nx):
        xx = (x + dx) % nx
        arrived(gxr.at[xx], q_r.at[xx])
        out = out + gxr[xx].astype(F32)
    gradx_ref[...] = out.astype(BF16)

    for dt in range(1, nt):
        tt = (tok + dt) % nt
        arrived(agb.at[tt], ag_r.at[tt])
    for tt in range(nt):
        ref, r0 = (grada_ref if tt % NC else gradb_ref), tt // NC * ra
        back = agb[tt].astype(F32)
        ref[r0:r0 + ra, 0:BLK] = back[0:ra]
        ref[r0:r0 + ra, BLK:2 * BLK] = back[ra:2 * ra]
        gradblk_ref[tt * rb:(tt + 1) * rb, :] = back[2 * ra:2 * ra + rb]

    for cond, copy in pending:
        if cond is None:
            copy.wait_send()
        else:
            pl.when(cond)(copy.wait_send)


def write_out(*refs):
    n = 5
    load, store = refs[3 * n], refs[3 * n + 1]
    ins = [pltpu.make_async_copy(refs[i], refs[2 * n + i], load.at[i]) for i in range(n)]
    outs = [pltpu.make_async_copy(refs[2 * n + i], refs[n + i], store.at[i]) for i in range(n)]
    for copy in ins:
        copy.start()
    for i in range(n):
        ins[i].wait()
        outs[i].start()
    for copy in outs:
        copy.wait()


def make(dims):
    nx, ny, nz = dims
    nq, nt = ny // nx, ny * NC

    def on_device(activations, w_base, blk_vals, blk_index, blk_count, a_down, b_up, grad_out):
        hb, fb = activations.shape
        nsl, rank = blk_vals.shape[0], a_down.shape[1]
        scale = float(hb * nt) ** (-0.5)
        ra, rb = rank // ny, nsl * BLK // nt
        dma = pltpu.SemaphoreType.DMA
        vmem = pltpu.VMEM
        shapes = [
            jax.ShapeDtypeStruct((hb, fb), BF16),
            jax.ShapeDtypeStruct((hb, fb), BF16),
            jax.ShapeDtypeStruct((rank, fb), F32),
            jax.ShapeDtypeStruct((rank, fb), F32),
            jax.ShapeDtypeStruct((nsl * BLK, BLK), F32),
        ]
        results = pl.pallas_call(
            functools.partial(kernel, dims, scale),
            out_shape=shapes,
            in_specs=[pl.BlockSpec(memory_space=pltpu.HBM)] * 8,
            out_specs=[pl.BlockSpec(memory_space=vmem)] * 5,
            scratch_shapes=[
                vmem((hb, fb), BF16), vmem((fb, 2 * fb), BF16), vmem((nsl, BLK, BLK), BF16), vmem((2, nsl), jnp.int32),
                vmem((1, 1), jnp.int32), vmem((rank, fb), BF16), vmem((rank, fb), BF16), vmem((hb, fb), BF16),
                vmem((ny + 1, 2, fb, fb), BF16),
                vmem((nx, nq, 2, fb, fb), BF16),
                vmem((nx, NC * hb, fb), BF16),
                vmem((nq, 2, NC * hb, fb), BF16),
                vmem((nz, hb, fb), BF16),
                vmem((2 * nq, NC * hb, fb), BF16),
                vmem((nx, hb, fb), BF16),
                vmem((nx, hb, fb), BF16),
                vmem((nx, NC * hb, fb), F32),
                vmem((nx, hb, fb), BF16),
                vmem((nx, hb, fb), BF16),
                vmem((nx, hb // nx, 2 * rank), BF16),
                vmem((nx, hb // nx, 2 * rank), BF16),
                vmem((nz, hb // nx, 2 * rank), BF16),
                vmem((nx, hb // nx, 2 * rank), BF16),
                vmem((hb, 2 * rank), BF16),
                vmem((nx, 8, BLK), F32),
                vmem((nx, nsl * BLK, BLK), F32),
                vmem((nx // NC, nsl * BLK, BLK), BF16),
                vmem((nx // NC, nsl * BLK, BLK), BF16),
                vmem((rank, fb), BF16),
                vmem((rank, fb), BF16),
                vmem((nx // NC, NC, rb, BLK), BF16),
                vmem((nx, rb, BLK), BF16),
                vmem((2 * ra + rb, BLK), F32),
                vmem((ny, 2 * ra + nx * rb, BLK), BF16),
                vmem((ny, 2 * ra + nx * rb, BLK), BF16),
                vmem((nt, 2 * ra + rb, BLK), BF16),
                vmem((4, 2 * rank, fb), BF16),
                vmem((2 * rank, fb), F32),
                dma((8,)),
                dma((2, ny)), dma((2, ny)),
                dma((ny + 1, 2)), dma((nx, nq, 2)),
                dma((nx,)),
                dma((nx,)), dma((nx,)),
                dma((nx,)), dma((nx,)),
                dma((nz,)), dma((nq, 2, NC)),
                dma((2 * nq, NC)), dma((nz,)),
                dma((nx,)), dma((nx,)),
                dma((1,)), dma((1,)),
                dma((nx,)), dma((nx,)),
                dma((nz,)), dma((nz,)),
                dma((nx,)), dma((nx,)),
                dma((nx,)), dma((nx,)),
                dma((2,)), dma((2,)),
                dma((nx // NC, NC)), dma((nx,)),
                dma((ny,)), dma((ny,)),
                dma((nt,)), dma((nt,)),
            ],
            compiler_params=pltpu.CompilerParams(
                collective_id=0, has_side_effects=True, vmem_limit_bytes=63 * 1024 * 1024
            ),
        )(activations, w_base, blk_vals, blk_index.T, blk_count.reshape(1, 1), a_down.T, b_up, grad_out)
        proj, gradx, grad_at, grad_b, blk = pl.pallas_call(
            write_out,
            out_shape=shapes,
            in_specs=[pl.BlockSpec(memory_space=pltpu.HBM)] * 5,
            out_specs=[pl.BlockSpec(memory_space=pltpu.HBM)] * 5,
            scratch_shapes=[vmem(s.shape, s.dtype) for s in shapes] + [dma((5,)), dma((5,))],
            compiler_params=pltpu.CompilerParams(vmem_limit_bytes=63 * 1024 * 1024),
        )(*results)
        return proj, gradx, blk.reshape(nsl, BLK, BLK), grad_at.T, grad_b

    return on_device


def solution(mesh, dims=(4, 8, 8)):
    in_specs = (
        P("tok", "feat"),
        P("feat", "tok"),
        P("feat", None, None),
        P("feat", None),
        P("feat"),
        P("feat", None),
        P(None, "feat"),
        P("tok", "feat"),
    )
    out_specs = (
        P("tok", "feat"),
        P("tok", "feat"),
        P("feat", None, None),
        P("feat", None),
        P(None, "feat"),
    )
    return jax.shard_map(make(dims), mesh=mesh, in_specs=in_specs, out_specs=out_specs, check_vma=False)
```

```python
import functools

import jax
import jax.numpy as jnp
from jax import lax
from jax.experimental import pallas as pl
from jax.experimental.pallas import tpu as pltpu
from jax.sharding import PartitionSpec as P

MESH = pl.DeviceIdType.MESH
F32 = jnp.float32
BF16 = jnp.bfloat16
BLK = 128
NC = 2


def dot(a, b, ca, cb):
    return lax.dot_general(a, b, (((ca,), (cb,)), ((), ())), preferred_element_type=F32)


def kernel(
    dims, scale,
    x_in, w_in, blk_in, index_in, count_in, at_in, b_in, g_in,
    proj_ref, gradx_ref, grada_ref, gradb_ref, gradblk_ref,
    x_ref, w_ref, blk_ref, index_ref, count_ref, at_ref, b_ref, g_ref,
    wl, wq, xg, gz, orx, os_, gxr, gxs, gxacc, gss, gsr, up, ux, uz, ut, ug, idxg, bs, bss, bsr, gas, gar, bx, br, tot, rss, rsr, agb, ab, gab,
    load_s, ring_s, ring_r, fwd_s, fwd_r, far_s, x_s, x_r, y_s, y_r, g_s, g_r, o_s, o_r, q_s, q_r, gs_s, gs_r,
    ux_s, ux_r, uz_s, uz_r, ug_s, ug_r, id_s, id_r, bc_s, bc_r, b_s, b_r, rs_s, rs_r, ag_s, ag_r,
):
    nx, ny, nz = dims
    nq = ny // nx
    nt = ny * NC
    half = ny // 2
    feat, tok = lax.axis_index("feat"), lax.axis_index("tok")
    x, z = feat // nz, feat % nz
    y, c = tok // NC, tok % NC
    zc = (z // 2) % 2
    zq, zh = z // (2 * NC), z % 2
    sib = 1 - c
    hb = x_ref.shape[0]
    pending = []

    def dev(xx, yy, zz, cc):
        return (xx * nz + zz, yy * NC + cc)

    def remote(src, dst, s_sem, r_sem, target):
        return pltpu.make_async_remote_copy(
            src_ref=src, dst_ref=dst, send_sem=s_sem, recv_sem=r_sem, device_id=target, device_id_type=MESH
        )

    def send(src, dst, s_sem, r_sem, target):
        copy = remote(src, dst, s_sem, r_sem, target)
        copy.start()
        pending.append((None, copy))

    def send_if(cond, src, dst, s_sem, r_sem, target):
        copy = remote(src, dst, s_sem, r_sem, target)
        pl.when(cond)(copy.start)
        pending.append((cond, copy))

    def send_or_keep(mine, src, dst, s_sem, r_sem, target):
        pl.when(mine)(pltpu.make_async_copy(src, dst, r_sem).start)
        send_if(jnp.logical_not(mine), src, dst, s_sem, r_sem, target)

    def arrived(dst, sem):
        pltpu.make_async_copy(dst, dst, sem).wait()

    barrier = pltpu.get_barrier_semaphore()
    greeted = 0
    for dz in range(1, nz):
        for cc in range(NC):
            pl.semaphore_signal(barrier, inc=1, device_id=dev(x, y, (z + dz) % nz, cc), device_id_type=MESH)
            greeted += 1
    for dt in range(1, nt):
        pl.semaphore_signal(barrier, inc=1, device_id=(feat, (tok + dt) % nt), device_id_type=MESH)
        greeted += 1
    for dx in range(1, nx):
        for cc in range(NC):
            pl.semaphore_signal(barrier, inc=1, device_id=dev((x + dx) % nx, y, z, cc), device_id_type=MESH)
            greeted += 1

    loads = []
    pairs = [
        (w_in, w_ref), (blk_in, blk_ref), (index_in, index_ref), (count_in, count_ref),
        (x_in, x_ref), (at_in, at_ref), (g_in, g_ref), (b_in, b_ref),
    ]
    for i, (src, dst) in enumerate(pairs):
        copy = pltpu.make_async_copy(src, dst, load_s.at[i])
        copy.start()
        loads.append(copy)
    for copy in loads[:4]:
        copy.wait()

    nsl = blk_ref.shape[0]
    for j in range(nsl):
        col = jnp.where(count_ref[...] > j, index_ref[1:2, j:j + 1], -1).astype(F32)
        idxg[x, j:j + 1, :] = jnp.broadcast_to(col, (1, BLK))
        idxg[x, 4 + j:5 + j, :] = jnp.broadcast_to(index_ref[0:1, j:j + 1].astype(F32), (1, BLK))
    for h in range(2):
        for rr in range(2):
            for hh in range(2):
                r0, c0 = rr * BLK, h * 2 * BLK + hh * BLK
                piece = w_ref[r0:r0 + BLK, c0:c0 + BLK].astype(F32)
                column = (tok * 4 + h * 2 + hh).astype(F32)
                for j in range(nsl):
                    hit = jnp.where(idxg[x, j:j + 1, :] == column, 1.0, 0.0) * jnp.where(
                        idxg[x, 4 + j:5 + j, :] == float(rr), 1.0, 0.0
                    )
                    piece = piece + hit * blk_ref[j].astype(F32)
                wl[0, h, r0:r0 + BLK, hh * BLK:(hh + 1) * BLK] = piece.astype(BF16)

    for copy in loads[4:]:
        copy.wait()
    rank = at_ref.shape[0]
    ab[...] = jnp.zeros_like(ab)
    ab[0, 0:rank, :] = at_ref[...]
    ab[1, rank:2 * rank, :] = b_ref[...]
    ab[2, 0:rank, :] = b_ref[...]
    ab[3, rank:2 * rank, :] = at_ref[...]
    part = (dot(x_ref[...], ab[0], 1, 1) + dot(g_ref[...], ab[1], 1, 1)).astype(BF16)
    ur = hb // nx
    for xx in range(nx):
        up[xx] = part[xx * ur:(xx + 1) * ur]

    pl.semaphore_wait(barrier, greeted)

    last = ny - 2

    def ring_slot(direction, k):
        d, sub = k // 2 + 1, (k + direction) % 2
        return (d if direction == 0 else half + d), d, sub

    def ring_send(direction, k):
        if k > last:
            return
        if k < 2:
            src = wl.at[0, (k + direction) % 2]
        else:
            slot, _, sub = ring_slot(direction, k - 2)
            src = wl.at[slot, sub]
        slot, _, sub = ring_slot(direction, k)
        to = (y + 1) % ny if direction == 0 else (y + ny - 1) % ny
        send(src, wl.at[slot, sub], ring_s.at[direction, k], ring_r.at[direction, k], dev(x, to, z, c))

    home = x == y // nq

    def hand_on(slot, sub, yy):
        xx, qq = yy // nq, yy % nq
        if far(slot, sub):
            pl.when(x == xx)(pltpu.make_async_copy(wl.at[slot, sub], wq.at[x, qq, sub], fwd_r.at[x, qq, sub]).start)
            return
        send_or_keep(
            x == xx, wl.at[slot, sub], wq.at[x, qq, sub], fwd_s.at[slot, sub], fwd_r.at[x, qq, sub], dev(xx, y, z, c)
        )

    def far(slot, sub):
        return nx == 4 and slot == 2 * half and sub == 1

    def to_far_row():
        qq = y % nq
        for dx in range(1, nx):
            xx = (x + dx) % nx
            piece = wq.at[xx, qq, 1]
            pl.when(home)(pltpu.make_async_copy(piece, piece, fwd_r.at[xx, qq, 1]).wait)
            send_if(home, piece, piece, far_s.at[dx], fwd_r.at[xx, qq, 1], dev(x, (y + half) % ny, z, c))

    def row_of(direction, d):
        return (y + ny - d) % ny if direction == 0 else (y + d) % ny

    def ring_step(k):
        for direction in range(2):
            slot, d, sub = ring_slot(direction, k)
            arrived(wl.at[slot, sub], ring_r.at[direction, k])
            ring_send(direction, k + 2)
            if k != ny - 3:
                hand_on(slot, sub, row_of(direction, d))
        if k == ny - 2 and k:
            for direction in range(2):
                slot, d, sub = ring_slot(direction, k - 1)
                hand_on(slot, sub, row_of(direction, d))

    mine_rows = pl.ds(pl.multiple_of(c * hb, hb), hb)
    for k in range(2):
        for direction in range(2):
            ring_send(direction, k)
    for dx in range(1, nx):
        xx = (x + dx) % nx
        send(up.at[xx], ux.at[x], ux_s.at[dx], ux_r.at[x], dev(xx, y, z, c))
        send(idxg.at[x], idxg.at[x], id_s.at[dx], id_r.at[x], dev(xx, y, z, c))
    for dx in range(1, nx):
        send(x_ref, xg.at[x, mine_rows], x_s.at[dx], x_r.at[x], dev((x + dx) % nx, y, z, c))
    pltpu.make_async_copy(x_ref, xg.at[x, mine_rows], x_r.at[x]).start()
    for h in range(2):
        hand_on(0, h, y)

    def low_rank_over_z():
        total = up[x].astype(F32)
        for dx in range(1, nx):
            xx = (x + dx) % nx
            arrived(ux.at[xx], ux_r.at[xx])
            total = total + ux[xx].astype(F32)
        uz[z] = total.astype(BF16)
        for dz in range(1, nz):
            send(uz.at[z], uz.at[z], uz_s.at[dz], uz_r.at[z], dev(x, y, (z + dz) % nz, c))

    def cotangent_over_z(distances):
        for dz in distances:
            args = (g_ref, gz.at[zq, zh, mine_rows], g_s.at[dz], g_r.at[zq, zh, c], dev(x, y, (z + dz) % nz, zc))
            if dz:
                send(*args)
            else:
                send_or_keep(c == zc, *args)

    def activations_on_chip():
        for dx in range(nx):
            xx = (x + dx) % nx
            arrived(xg.at[xx, mine_rows], x_r.at[xx])
            send(xg.at[xx, mine_rows], xg.at[xx, mine_rows], y_s.at[xx], y_r.at[xx], dev(x, y, z, sib))

    def low_rank_over_x():
        total = uz[z].astype(F32)
        for dz in range(1, nz):
            zz = (z + dz) % nz
            arrived(uz.at[zz], uz_r.at[zz])
            total = total + uz[zz].astype(F32)
        ut[x] = total.astype(BF16)
        for dx in range(1, nx):
            send(ut.at[x], ut.at[x], ug_s.at[dx], ug_r.at[x], dev((x + dx) % nx, y, z, c))

    def low_rank_done():
        for dx in range(1, nx):
            xx = (x + dx) % nx
            arrived(ut.at[xx], ug_r.at[xx])
        for xx in range(nx):
            ug[xx * ur:(xx + 1) * ur, :] = ut[xx]
        uv = ug[...]
        gab[0:rank] = dot(uv, g_ref[...], 0, 0)[0:rank]
        gab[rank:2 * rank] = dot(uv, x_ref[...], 0, 0)[rank:2 * rank]

    def blocks_over_x():
        other_rows = pl.ds(pl.multiple_of(sib * hb, hb), hb)
        for dx in range(nx):
            xx = (x + dx) % nx
            if dx:
                arrived(idxg.at[xx], id_r.at[xx])
            arrived(xg.at[xx, other_rows], y_r.at[xx])
        for qq in range(nq):
            for h in range(2):
                for cc in range(NC):
                    arrived(gz.at[qq, h, cc * hb:(cc + 1) * hb], g_r.at[qq, h, cc])
        for dx in range(nx):
            xx = (x + dx) % nx
            for j in range(nsl):
                col, row = idxg[xx, j:j + 1, :], idxg[xx, 4 + j:5 + j, :]
                picked = jnp.zeros((NC * hb, BLK), BF16)
                for qq in range(nq):
                    for h in range(2):
                        base = (2 * (x * nz + 4 * qq + 2 * c + h)).astype(F32)
                        for hh in range(2):
                            hit = jnp.where(col == base + float(hh), 1.0, 0.0).astype(BF16)
                            picked = picked + gz[qq, h, :, hh * BLK:(hh + 1) * BLK] * hit
                top = jnp.where(row == 0.0, 1.0, 0.0).astype(BF16)
                low = jnp.where(row == 1.0, 1.0, 0.0).astype(BF16)
                xs = xg[xx, :, 0:BLK] * top + xg[xx, :, BLK:2 * BLK] * low
                bs[dx, j * BLK:(j + 1) * BLK, :] = dot(xs, picked, 0, 0)

    ra, rb = rank // ny, nsl * BLK // nt
    hx = nx // NC

    def blocks_on_chip():
        for i in range(hx):
            bss[i] = bs[sib * hx + i].astype(BF16)
        send(bss, bsr, bc_s.at[0], bc_r.at[0], dev(x, y, z, sib))

    def low_rank_on_chip():
        gas[...] = gab[pl.ds(pl.multiple_of(sib * rank, rank), rank)].astype(BF16)
        send(gas, gar, bc_s.at[1], bc_r.at[1], dev(x, y, z, sib))

    def grads_over_tok():
        arrived(bsr, bc_r.at[0])
        for i in range(hx):
            rows = bs[c * hx + i] + bsr[i].astype(F32)
            for yy in range(ny):
                r0 = 2 * ra + i * NC * rb
                rss[yy, r0:r0 + NC * rb, :] = rows[yy * NC * rb:(yy + 1) * NC * rb].astype(BF16)
        arrived(gar, bc_r.at[1])
        sums = gab[pl.ds(pl.multiple_of(c * rank, rank), rank)] + gar[...].astype(F32)
        for yy in range(ny):
            rows = sums[yy * ra:(yy + 1) * ra]
            rss[yy, 0:2 * ra, :] = jnp.concatenate([rows[:, 0:BLK], rows[:, BLK:2 * BLK]], axis=0).astype(BF16)
        rsr[y] = rss[y]
        for dy in range(1, ny):
            yy = (y + dy) % ny
            send(rss.at[yy], rsr.at[y], rs_s.at[dy], rs_r.at[y], dev(x, yy, z, c))

    def blocks_home():
        total = rsr[y].astype(F32)
        for dy in range(1, ny):
            yy = (y + dy) % ny
            arrived(rsr.at[yy], rs_r.at[yy])
            total = total + rsr[yy].astype(F32)
        tot[0:2 * ra, :] = total[0:2 * ra]
        for i in range(hx):
            xx = (x + c * hx + i) % nx
            for cc in range(NC):
                r0 = 2 * ra + (i * NC + cc) * rb
                bx[i, cc] = total[r0:r0 + rb].astype(BF16)
                args = (bx.at[i, cc], br.at[x], b_s.at[i, cc], b_r.at[x], dev(xx, y, z, cc))
                if i == 0 and cc == 0:
                    send_or_keep(c == 0, *args)
                else:
                    send(*args)

    def grads_back():
        total = jnp.zeros((rb, BLK), F32)
        for xx in range(nx):
            arrived(br.at[xx], b_r.at[xx])
            total = total + br[xx].astype(F32)
        tot[2 * ra:2 * ra + rb, :] = total
        agb[tok] = (tot[...] * scale).astype(BF16)
        for dt in range(1, nt):
            send(agb.at[tok], agb.at[tok], ag_s.at[dt], ag_r.at[tok], (feat, (tok + dt) % nt))

    def chunk(step):
        if nq == 1:
            qq, h = 0, step
        else:
            away = (x + nx - y // nq) % nx
            first = jnp.where(away == 2, 1 - y % 2, jnp.where(away == 3, 1, 0))
            if step % 2:
                qq, h = 1 - first, (jnp.where(away == 1, 1, 0) + step // 2) % 2
            else:
                qq, h = first, (jnp.where(away == 2, y % 2, 0) + step // 2) % 2
        early = jnp.logical_and(home, jnp.logical_and(qq == y % nq, h == 1)) if nx == 4 else None
        for dx in range(nx):
            xx = (x + dx) % nx
            piece = wq.at[xx, qq, h]
            if dx and nx == 4:
                pl.when(jnp.logical_not(early))(pltpu.make_async_copy(piece, piece, fwd_r.at[xx, qq, h]).wait)
            else:
                arrived(piece, fwd_r.at[xx, qq, h])
        out = dot(xg[0], wq[0, qq, h], 1, 0)
        for xx in range(1, nx):
            out = out + dot(xg[xx], wq[xx, qq, h], 1, 0)
        os_[step] = out.astype(BF16)
        zz = 4 * qq + 2 * c + h
        for cc in range(NC):
            send_or_keep(
                jnp.logical_and(z == zz, c == cc),
                os_.at[step, cc * hb:(cc + 1) * hb], orx.at[z], o_s.at[step, cc], o_r.at[z], dev(x, y, zz, cc),
            )
        for xx in range(nx):
            term = dot(gz[qq, h], wq[xx, qq, h], 1, 1)
            gxacc[xx] = term if step == 0 else gxacc[xx] + term

    def inputs_on_chip():
        other_rows = pl.ds(pl.multiple_of(sib * hb, hb), hb)
        gss[...] = gxacc[:, other_rows, :].astype(BF16)
        send(gss, gsr, gs_s.at[0], gs_r.at[0], dev(x, y, z, sib))

    def inputs_over_x():
        arrived(gsr, gs_r.at[0])
        for dx in range(nx):
            xx = (x + dx) % nx
            gxs[dx] = (gxacc[xx, mine_rows, :] + gsr[xx].astype(F32)).astype(BF16)
            if dx:
                send(gxs.at[dx], gxr.at[x], q_s.at[dx], q_r.at[x], dev(xx, y, z, c))

    around = sorted(range(nz), key=lambda dz: -min(dz, nz - dz))
    cotangent_over_z(around[:3])
    low_rank_over_z()
    cotangent_over_z(around[3:])
    after = {1: [activations_on_chip], 2: [low_rank_over_x], ny - 4: [to_far_row] if nx == 4 else [], ny - 3: [blocks_over_x, blocks_on_chip]}
    for k in range(ny - 1):
        ring_step(k)
        for side in after.pop(k, []):
            side()
    for k in sorted(after):
        for side in after[k]:
            side()
    low_rank_done()
    low_rank_on_chip()
    grads_over_tok()
    for step in range(2 * nq):
        chunk(step)
        if step == nq - 1:
            blocks_home()
    inputs_on_chip()
    grads_back()
    inputs_over_x()

    uv = ug[...]
    out = dot(uv, ab[2], 1, 0)
    for zz in range(nz):
        arrived(orx.at[zz], o_r.at[zz])
        out = out + orx[zz].astype(F32)
    proj_ref[...] = out.astype(BF16)

    out = dot(uv, ab[3], 1, 0) + gxs[0].astype(F32)
    for dx in range(1, nx):
        xx = (x + dx) % nx
        arrived(gxr.at[xx], q_r.at[xx])
        out = out + gxr[xx].astype(F32)
    gradx_ref[...] = out.astype(BF16)

    for dt in range(1, nt):
        tt = (tok + dt) % nt
        arrived(agb.at[tt], ag_r.at[tt])
    for tt in range(nt):
        ref, r0 = (grada_ref if tt % NC else gradb_ref), tt // NC * ra
        back = agb[tt].astype(F32)
        ref[r0:r0 + ra, 0:BLK] = back[0:ra]
        ref[r0:r0 + ra, BLK:2 * BLK] = back[ra:2 * ra]
        gradblk_ref[tt * rb:(tt + 1) * rb, :] = back[2 * ra:2 * ra + rb]

    for cond, copy in pending:
        if cond is None:
            copy.wait_send()
        else:
            pl.when(cond)(copy.wait_send)


def write_out(*refs):
    n = 5
    load, store = refs[3 * n], refs[3 * n + 1]
    ins = [pltpu.make_async_copy(refs[i], refs[2 * n + i], load.at[i]) for i in range(n)]
    outs = [pltpu.make_async_copy(refs[2 * n + i], refs[n + i], store.at[i]) for i in range(n)]
    for copy in ins:
        copy.start()
    for i in range(n):
        ins[i].wait()
        outs[i].start()
    for copy in outs:
        copy.wait()


def make(dims):
    nx, ny, nz = dims
    nq, nt = ny // nx, ny * NC

    def on_device(activations, w_base, blk_vals, blk_index, blk_count, a_down, b_up, grad_out):
        hb, fb = activations.shape
        nsl, rank = blk_vals.shape[0], a_down.shape[1]
        scale = float(hb * nt) ** (-0.5)
        ra, rb = rank // ny, nsl * BLK // nt
        dma = pltpu.SemaphoreType.DMA
        vmem = pltpu.VMEM
        shapes = [
            jax.ShapeDtypeStruct((hb, fb), BF16),
            jax.ShapeDtypeStruct((hb, fb), BF16),
            jax.ShapeDtypeStruct((rank, fb), F32),
            jax.ShapeDtypeStruct((rank, fb), F32),
            jax.ShapeDtypeStruct((nsl * BLK, BLK), F32),
        ]
        results = pl.pallas_call(
            functools.partial(kernel, dims, scale),
            out_shape=shapes,
            in_specs=[pl.BlockSpec(memory_space=pltpu.HBM)] * 8,
            out_specs=[pl.BlockSpec(memory_space=vmem)] * 5,
            scratch_shapes=[
                vmem((hb, fb), BF16), vmem((fb, 2 * fb), BF16), vmem((nsl, BLK, BLK), BF16), vmem((2, nsl), jnp.int32),
                vmem((1, 1), jnp.int32), vmem((rank, fb), BF16), vmem((rank, fb), BF16), vmem((hb, fb), BF16),
                vmem((ny + 1, 2, fb, fb), BF16),
                vmem((nx, nq, 2, fb, fb), BF16),
                vmem((nx, NC * hb, fb), BF16),
                vmem((nq, 2, NC * hb, fb), BF16),
                vmem((nz, hb, fb), BF16),
                vmem((2 * nq, NC * hb, fb), BF16),
                vmem((nx, hb, fb), BF16),
                vmem((nx, hb, fb), BF16),
                vmem((nx, NC * hb, fb), F32),
                vmem((nx, hb, fb), BF16),
                vmem((nx, hb, fb), BF16),
                vmem((nx, hb // nx, 2 * rank), BF16),
                vmem((nx, hb // nx, 2 * rank), BF16),
                vmem((nz, hb // nx, 2 * rank), BF16),
                vmem((nx, hb // nx, 2 * rank), BF16),
                vmem((hb, 2 * rank), BF16),
                vmem((nx, 8, BLK), F32),
                vmem((nx, nsl * BLK, BLK), F32),
                vmem((nx // NC, nsl * BLK, BLK), BF16),
                vmem((nx // NC, nsl * BLK, BLK), BF16),
                vmem((rank, fb), BF16),
                vmem((rank, fb), BF16),
                vmem((nx // NC, NC, rb, BLK), BF16),
                vmem((nx, rb, BLK), BF16),
                vmem((2 * ra + rb, BLK), F32),
                vmem((ny, 2 * ra + nx * rb, BLK), BF16),
                vmem((ny, 2 * ra + nx * rb, BLK), BF16),
                vmem((nt, 2 * ra + rb, BLK), BF16),
                vmem((4, 2 * rank, fb), BF16),
                vmem((2 * rank, fb), F32),
                dma((8,)),
                dma((2, ny)), dma((2, ny)),
                dma((ny + 1, 2)), dma((nx, nq, 2)),
                dma((nx,)),
                dma((nx,)), dma((nx,)),
                dma((nx,)), dma((nx,)),
                dma((nz,)), dma((nq, 2, NC)),
                dma((2 * nq, NC)), dma((nz,)),
                dma((nx,)), dma((nx,)),
                dma((1,)), dma((1,)),
                dma((nx,)), dma((nx,)),
                dma((nz,)), dma((nz,)),
                dma((nx,)), dma((nx,)),
                dma((nx,)), dma((nx,)),
                dma((2,)), dma((2,)),
                dma((nx // NC, NC)), dma((nx,)),
                dma((ny,)), dma((ny,)),
                dma((nt,)), dma((nt,)),
            ],
            compiler_params=pltpu.CompilerParams(
                collective_id=0, has_side_effects=True, vmem_limit_bytes=63 * 1024 * 1024
            ),
        )(activations, w_base, blk_vals, blk_index.T, blk_count.reshape(1, 1), a_down.T, b_up, grad_out)
        proj, gradx, grad_at, grad_b, blk = pl.pallas_call(
            write_out,
            out_shape=shapes,
            in_specs=[pl.BlockSpec(memory_space=pltpu.HBM)] * 5,
            out_specs=[pl.BlockSpec(memory_space=pltpu.HBM)] * 5,
            scratch_shapes=[vmem(s.shape, s.dtype) for s in shapes] + [dma((5,)), dma((5,))],
            compiler_params=pltpu.CompilerParams(vmem_limit_bytes=63 * 1024 * 1024),
        )(*results)
        return proj, gradx, blk.reshape(nsl, BLK, BLK), grad_at.T, grad_b

    return on_device


def solution(mesh, dims=(4, 8, 8)):
    in_specs = (
        P("tok", "feat"),
        P("feat", "tok"),
        P("feat", None, None),
        P("feat", None),
        P("feat"),
        P("feat", None),
        P(None, "feat"),
        P("tok", "feat"),
    )
    out_specs = (
        P("tok", "feat"),
        P("tok", "feat"),
        P("feat", None, None),
        P("feat", None),
        P(None, "feat"),
    )
    return jax.shard_map(make(dims), mesh=mesh, in_specs=in_specs, out_specs=out_specs, check_vma=False)
```

```python
import functools

import jax
import jax.numpy as jnp
from jax import lax
from jax.experimental import pallas as pl
from jax.experimental.pallas import tpu as pltpu
from jax.sharding import PartitionSpec as P

MESH = pl.DeviceIdType.MESH
F32 = jnp.float32
BF16 = jnp.bfloat16
BLK = 128
NC = 2


def dot(a, b, ca, cb):
    return lax.dot_general(a, b, (((ca,), (cb,)), ((), ())), preferred_element_type=F32)


def kernel(
    dims, scale,
    x_in, w_in, blk_in, index_in, count_in, at_in, b_in, g_in,
    proj_ref, gradx_ref, grada_ref, gradb_ref, gradblk_ref,
    x_ref, w_ref, blk_ref, index_ref, count_ref, at_ref, b_ref, g_ref,
    wl, wq, xg, gz, orx, os_, gxr, gxs, gxacc, gss, gsr, up, ux, uz, ut, ug, idxg, bs, bss, bsr, gas, gar, bx, br, tot, rss, rsr, agb, ab, gab,
    load_s, ring_s, ring_r, fwd_s, fwd_r, far_s, x_s, x_r, y_s, y_r, g_s, g_r, o_s, o_r, q_s, q_r, gs_s, gs_r,
    ux_s, ux_r, uz_s, uz_r, ug_s, ug_r, id_s, id_r, bc_s, bc_r, b_s, b_r, rs_s, rs_r, ag_s, ag_r,
):
    nx, ny, nz = dims
    nq = ny // nx
    nt = ny * NC
    half = ny // 2
    feat, tok = lax.axis_index("feat"), lax.axis_index("tok")
    x, z = feat // nz, feat % nz
    y, c = tok // NC, tok % NC
    zc = (z // 2) % 2
    zq, zh = z // (2 * NC), z % 2
    sib = 1 - c
    hb = x_ref.shape[0]
    pending = []

    def dev(xx, yy, zz, cc):
        return (xx * nz + zz, yy * NC + cc)

    def remote(src, dst, s_sem, r_sem, target):
        return pltpu.make_async_remote_copy(
            src_ref=src, dst_ref=dst, send_sem=s_sem, recv_sem=r_sem, device_id=target, device_id_type=MESH
        )

    def send(src, dst, s_sem, r_sem, target):
        copy = remote(src, dst, s_sem, r_sem, target)
        copy.start()
        pending.append((None, copy))

    def send_if(cond, src, dst, s_sem, r_sem, target):
        copy = remote(src, dst, s_sem, r_sem, target)
        pl.when(cond)(copy.start)
        pending.append((cond, copy))

    def send_or_keep(mine, src, dst, s_sem, r_sem, target):
        pl.when(mine)(pltpu.make_async_copy(src, dst, r_sem).start)
        send_if(jnp.logical_not(mine), src, dst, s_sem, r_sem, target)

    def arrived(dst, sem):
        pltpu.make_async_copy(dst, dst, sem).wait()

    barrier = pltpu.get_barrier_semaphore()
    greeted = 0
    for dz in range(1, nz):
        for cc in range(NC):
            pl.semaphore_signal(barrier, inc=1, device_id=dev(x, y, (z + dz) % nz, cc), device_id_type=MESH)
            greeted += 1
    for dt in range(1, nt):
        pl.semaphore_signal(barrier, inc=1, device_id=(feat, (tok + dt) % nt), device_id_type=MESH)
        greeted += 1
    for dx in range(1, nx):
        for cc in range(NC):
            pl.semaphore_signal(barrier, inc=1, device_id=dev((x + dx) % nx, y, z, cc), device_id_type=MESH)
            greeted += 1

    loads = []
    pairs = [
        (w_in, w_ref), (blk_in, blk_ref), (index_in, index_ref), (count_in, count_ref),
        (x_in, x_ref), (at_in, at_ref), (g_in, g_ref), (b_in, b_ref),
    ]
    for i, (src, dst) in enumerate(pairs):
        copy = pltpu.make_async_copy(src, dst, load_s.at[i])
        copy.start()
        loads.append(copy)
    for copy in loads[:4]:
        copy.wait()

    nsl = blk_ref.shape[0]
    for j in range(nsl):
        col = jnp.where(count_ref[...] > j, index_ref[1:2, j:j + 1], -1).astype(F32)
        idxg[x, j:j + 1, :] = jnp.broadcast_to(col, (1, BLK))
        idxg[x, 4 + j:5 + j, :] = jnp.broadcast_to(index_ref[0:1, j:j + 1].astype(F32), (1, BLK))
    for h in range(2):
        for rr in range(2):
            for hh in range(2):
                r0, c0 = rr * BLK, h * 2 * BLK + hh * BLK
                piece = w_ref[r0:r0 + BLK, c0:c0 + BLK].astype(F32)
                column = (tok * 4 + h * 2 + hh).astype(F32)
                for j in range(nsl):
                    hit = jnp.where(idxg[x, j:j + 1, :] == column, 1.0, 0.0) * jnp.where(
                        idxg[x, 4 + j:5 + j, :] == float(rr), 1.0, 0.0
                    )
                    piece = piece + hit * blk_ref[j].astype(F32)
                wl[0, h, r0:r0 + BLK, hh * BLK:(hh + 1) * BLK] = piece.astype(BF16)

    for copy in loads[4:]:
        copy.wait()
    rank = at_ref.shape[0]
    ab[...] = jnp.zeros_like(ab)
    ab[0, 0:rank, :] = at_ref[...]
    ab[1, rank:2 * rank, :] = b_ref[...]
    ab[2, 0:rank, :] = b_ref[...]
    ab[3, rank:2 * rank, :] = at_ref[...]
    part = (dot(x_ref[...], ab[0], 1, 1) + dot(g_ref[...], ab[1], 1, 1)).astype(BF16)
    ur = hb // nx
    for xx in range(nx):
        up[xx] = part[xx * ur:(xx + 1) * ur]

    pl.semaphore_wait(barrier, greeted)

    last = ny - 2

    def ring_slot(direction, k):
        d, sub = k // 2 + 1, (k + direction) % 2
        return (d if direction == 0 else half + d), d, sub

    def ring_send(direction, k):
        if k > last:
            return
        if k < 2:
            src = wl.at[0, (k + direction) % 2]
        else:
            slot, _, sub = ring_slot(direction, k - 2)
            src = wl.at[slot, sub]
        slot, _, sub = ring_slot(direction, k)
        to = (y + 1) % ny if direction == 0 else (y + ny - 1) % ny
        send(src, wl.at[slot, sub], ring_s.at[direction, k], ring_r.at[direction, k], dev(x, to, z, c))

    home = x == y // nq

    def hand_on(slot, sub, yy):
        xx, qq = yy // nq, yy % nq
        if far(slot, sub):
            pl.when(x == xx)(pltpu.make_async_copy(wl.at[slot, sub], wq.at[x, qq, sub], fwd_r.at[x, qq, sub]).start)
            return
        send_or_keep(
            x == xx, wl.at[slot, sub], wq.at[x, qq, sub], fwd_s.at[slot, sub], fwd_r.at[x, qq, sub], dev(xx, y, z, c)
        )

    def far(slot, sub):
        return nx == 4 and slot == 2 * half and sub == 1

    def to_far_row():
        qq = y % nq
        for dx in range(1, nx):
            xx = (x + dx) % nx
            piece = wq.at[xx, qq, 1]
            pl.when(home)(pltpu.make_async_copy(piece, piece, fwd_r.at[xx, qq, 1]).wait)
            send_if(home, piece, piece, far_s.at[dx], fwd_r.at[xx, qq, 1], dev(x, (y + half) % ny, z, c))

    def row_of(direction, d):
        return (y + ny - d) % ny if direction == 0 else (y + d) % ny

    def ring_step(k):
        for direction in range(2):
            slot, d, sub = ring_slot(direction, k)
            arrived(wl.at[slot, sub], ring_r.at[direction, k])
            ring_send(direction, k + 2)
            if k != ny - 3:
                hand_on(slot, sub, row_of(direction, d))
        if k == ny - 2 and k:
            for direction in range(2):
                slot, d, sub = ring_slot(direction, k - 1)
                hand_on(slot, sub, row_of(direction, d))

    mine_rows = pl.ds(pl.multiple_of(c * hb, hb), hb)
    for k in range(2):
        for direction in range(2):
            ring_send(direction, k)
    for dx in range(1, nx):
        xx = (x + dx) % nx
        send(up.at[xx], ux.at[x], ux_s.at[dx], ux_r.at[x], dev(xx, y, z, c))
        send(idxg.at[x], idxg.at[x], id_s.at[dx], id_r.at[x], dev(xx, y, z, c))
    for dx in range(1, nx):
        send(x_ref, xg.at[x, mine_rows], x_s.at[dx], x_r.at[x], dev((x + dx) % nx, y, z, c))
    pltpu.make_async_copy(x_ref, xg.at[x, mine_rows], x_r.at[x]).start()
    for h in range(2):
        hand_on(0, h, y)

    def low_rank_over_z():
        total = up[x].astype(F32)
        for dx in range(1, nx):
            xx = (x + dx) % nx
            arrived(ux.at[xx], ux_r.at[xx])
            total = total + ux[xx].astype(F32)
        uz[z] = total.astype(BF16)
        for dz in range(1, nz):
            send(uz.at[z], uz.at[z], uz_s.at[dz], uz_r.at[z], dev(x, y, (z + dz) % nz, c))

    def cotangent_over_z(distances):
        for dz in distances:
            args = (g_ref, gz.at[zq, zh, mine_rows], g_s.at[dz], g_r.at[zq, zh, c], dev(x, y, (z + dz) % nz, zc))
            if dz:
                send(*args)
            else:
                send_or_keep(c == zc, *args)

    def activations_on_chip():
        for dx in range(nx):
            xx = (x + dx) % nx
            arrived(xg.at[xx, mine_rows], x_r.at[xx])
            send(xg.at[xx, mine_rows], xg.at[xx, mine_rows], y_s.at[xx], y_r.at[xx], dev(x, y, z, sib))

    def low_rank_over_x():
        total = uz[z].astype(F32)
        for dz in range(1, nz):
            zz = (z + dz) % nz
            arrived(uz.at[zz], uz_r.at[zz])
            total = total + uz[zz].astype(F32)
        ut[x] = total.astype(BF16)
        for dx in range(1, nx):
            send(ut.at[x], ut.at[x], ug_s.at[dx], ug_r.at[x], dev((x + dx) % nx, y, z, c))

    def low_rank_done():
        for dx in range(1, nx):
            xx = (x + dx) % nx
            arrived(ut.at[xx], ug_r.at[xx])
        for xx in range(nx):
            ug[xx * ur:(xx + 1) * ur, :] = ut[xx]
        uv = ug[...]
        gab[0:rank] = dot(uv, g_ref[...], 0, 0)[0:rank]
        gab[rank:2 * rank] = dot(uv, x_ref[...], 0, 0)[rank:2 * rank]

    def blocks_over_x():
        other_rows = pl.ds(pl.multiple_of(sib * hb, hb), hb)
        for dx in range(nx):
            xx = (x + dx) % nx
            if dx:
                arrived(idxg.at[xx], id_r.at[xx])
            arrived(xg.at[xx, other_rows], y_r.at[xx])
        for qq in range(nq):
            for h in range(2):
                for cc in range(NC):
                    arrived(gz.at[qq, h, cc * hb:(cc + 1) * hb], g_r.at[qq, h, cc])
        for dx in range(nx):
            xx = (x + dx) % nx
            for j in range(nsl):
                col, row = idxg[xx, j:j + 1, :], idxg[xx, 4 + j:5 + j, :]
                picked = jnp.zeros((NC * hb, BLK), BF16)
                for qq in range(nq):
                    for h in range(2):
                        base = (2 * (x * nz + 4 * qq + 2 * c + h)).astype(F32)
                        for hh in range(2):
                            hit = jnp.where(col == base + float(hh), 1.0, 0.0).astype(BF16)
                            picked = picked + gz[qq, h, :, hh * BLK:(hh + 1) * BLK] * hit
                top = jnp.where(row == 0.0, 1.0, 0.0).astype(BF16)
                low = jnp.where(row == 1.0, 1.0, 0.0).astype(BF16)
                xs = xg[xx, :, 0:BLK] * top + xg[xx, :, BLK:2 * BLK] * low
                bs[dx, j * BLK:(j + 1) * BLK, :] = dot(xs, picked, 0, 0)

    ra, rb = rank // ny, nsl * BLK // nt
    hx = nx // NC

    def blocks_on_chip():
        for i in range(hx):
            bss[i] = bs[sib * hx + i].astype(BF16)
        send(bss, bsr, bc_s.at[0], bc_r.at[0], dev(x, y, z, sib))

    def low_rank_on_chip():
        gas[...] = gab[pl.ds(pl.multiple_of(sib * rank, rank), rank)].astype(BF16)
        send(gas, gar, bc_s.at[1], bc_r.at[1], dev(x, y, z, sib))

    def grads_over_tok():
        arrived(bsr, bc_r.at[0])
        for i in range(hx):
            rows = bs[c * hx + i] + bsr[i].astype(F32)
            for yy in range(ny):
                r0 = 2 * ra + i * NC * rb
                rss[yy, r0:r0 + NC * rb, :] = rows[yy * NC * rb:(yy + 1) * NC * rb].astype(BF16)
        arrived(gar, bc_r.at[1])
        sums = gab[pl.ds(pl.multiple_of(c * rank, rank), rank)] + gar[...].astype(F32)
        for yy in range(ny):
            rows = sums[yy * ra:(yy + 1) * ra]
            rss[yy, 0:2 * ra, :] = jnp.concatenate([rows[:, 0:BLK], rows[:, BLK:2 * BLK]], axis=0).astype(BF16)
        rsr[y] = rss[y]
        for dy in range(1, ny):
            yy = (y + dy) % ny
            send(rss.at[yy], rsr.at[y], rs_s.at[dy], rs_r.at[y], dev(x, yy, z, c))

    def blocks_home():
        total = rsr[y].astype(F32)
        for dy in range(1, ny):
            yy = (y + dy) % ny
            arrived(rsr.at[yy], rs_r.at[yy])
            total = total + rsr[yy].astype(F32)
        tot[0:2 * ra, :] = total[0:2 * ra]
        for i in range(hx):
            xx = (x + c * hx + i) % nx
            for cc in range(NC):
                r0 = 2 * ra + (i * NC + cc) * rb
                bx[i, cc] = total[r0:r0 + rb].astype(BF16)
                args = (bx.at[i, cc], br.at[x], b_s.at[i, cc], b_r.at[x], dev(xx, y, z, cc))
                if i == 0 and cc == 0:
                    send_or_keep(c == 0, *args)
                else:
                    send(*args)

    def grads_back():
        total = jnp.zeros((rb, BLK), F32)
        for xx in range(nx):
            arrived(br.at[xx], b_r.at[xx])
            total = total + br[xx].astype(F32)
        tot[2 * ra:2 * ra + rb, :] = total
        agb[tok] = (tot[...] * scale).astype(BF16)
        for dt in range(1, nt):
            send(agb.at[tok], agb.at[tok], ag_s.at[dt], ag_r.at[tok], (feat, (tok + dt) % nt))

    def chunk(step):
        if nq == 1:
            qq, h = 0, step
        else:
            away = (x + nx - y // nq) % nx
            first = jnp.where(away == 2, 1 - y % 2, jnp.where(away == 3, 1, 0))
            if step % 2:
                qq, h = 1 - first, (jnp.where(away == 1, 1, 0) + step // 2) % 2
            else:
                qq, h = first, (jnp.where(away == 2, y % 2, 0) + step // 2) % 2
        early = jnp.logical_and(home, jnp.logical_and(qq == y % nq, h == 1)) if nx == 4 else None
        for dx in range(nx):
            xx = (x + dx) % nx
            piece = wq.at[xx, qq, h]
            if dx and nx == 4:
                pl.when(jnp.logical_not(early))(pltpu.make_async_copy(piece, piece, fwd_r.at[xx, qq, h]).wait)
            else:
                arrived(piece, fwd_r.at[xx, qq, h])
        out = dot(xg[0], wq[0, qq, h], 1, 0)
        for xx in range(1, nx):
            out = out + dot(xg[xx], wq[xx, qq, h], 1, 0)
        os_[step] = out.astype(BF16)
        zz = 4 * qq + 2 * c + h
        for cc in range(NC):
            send_or_keep(
                jnp.logical_and(z == zz, c == cc),
                os_.at[step, cc * hb:(cc + 1) * hb], orx.at[z], o_s.at[step, cc], o_r.at[z], dev(x, y, zz, cc),
            )
        for xx in range(nx):
            term = dot(gz[qq, h], wq[xx, qq, h], 1, 1)
            gxacc[xx] = term if step == 0 else gxacc[xx] + term

    def inputs_on_chip():
        other_rows = pl.ds(pl.multiple_of(sib * hb, hb), hb)
        gss[...] = gxacc[:, other_rows, :].astype(BF16)
        send(gss, gsr, gs_s.at[0], gs_r.at[0], dev(x, y, z, sib))

    def inputs_over_x():
        arrived(gsr, gs_r.at[0])
        for dx in range(nx):
            xx = (x + dx) % nx
            gxs[dx] = (gxacc[xx, mine_rows, :] + gsr[xx].astype(F32)).astype(BF16)
            if dx:
                send(gxs.at[dx], gxr.at[x], q_s.at[dx], q_r.at[x], dev(xx, y, z, c))

    around = sorted(range(nz), key=lambda dz: -min(dz, nz - dz))
    cotangent_over_z(around[:3])
    low_rank_over_z()
    cotangent_over_z(around[3:])
    after = {1: [activations_on_chip], 2: [low_rank_over_x], ny - 4: [to_far_row] if nx == 4 else [], ny - 3: [blocks_over_x, blocks_on_chip]}
    for k in range(ny - 1):
        ring_step(k)
        for side in after.pop(k, []):
            side()
    for k in sorted(after):
        for side in after[k]:
            side()
    low_rank_done()
    low_rank_on_chip()
    grads_over_tok()
    for step in range(2 * nq):
        chunk(step)
        if step == nq - 1:
            blocks_home()
    grads_back()
    inputs_on_chip()
    inputs_over_x()

    uv = ug[...]
    out = dot(uv, ab[2], 1, 0)
    for zz in range(nz):
        arrived(orx.at[zz], o_r.at[zz])
        out = out + orx[zz].astype(F32)
    proj_ref[...] = out.astype(BF16)

    out = dot(uv, ab[3], 1, 0) + gxs[0].astype(F32)
    for dx in range(1, nx):
        xx = (x + dx) % nx
        arrived(gxr.at[xx], q_r.at[xx])
        out = out + gxr[xx].astype(F32)
    gradx_ref[...] = out.astype(BF16)

    for dt in range(1, nt):
        tt = (tok + dt) % nt
        arrived(agb.at[tt], ag_r.at[tt])
    for tt in range(nt):
        ref, r0 = (grada_ref if tt % NC else gradb_ref), tt // NC * ra
        back = agb[tt].astype(F32)
        ref[r0:r0 + ra, 0:BLK] = back[0:ra]
        ref[r0:r0 + ra, BLK:2 * BLK] = back[ra:2 * ra]
        gradblk_ref[tt * rb:(tt + 1) * rb, :] = back[2 * ra:2 * ra + rb]

    for cond, copy in pending:
        if cond is None:
            copy.wait_send()
        else:
            pl.when(cond)(copy.wait_send)


def write_out(*refs):
    n = 5
    load, store = refs[3 * n], refs[3 * n + 1]
    ins = [pltpu.make_async_copy(refs[i], refs[2 * n + i], load.at[i]) for i in range(n)]
    outs = [pltpu.make_async_copy(refs[2 * n + i], refs[n + i], store.at[i]) for i in range(n)]
    for copy in ins:
        copy.start()
    for i in range(n):
        ins[i].wait()
        outs[i].start()
    for copy in outs:
        copy.wait()


def make(dims):
    nx, ny, nz = dims
    nq, nt = ny // nx, ny * NC

    def on_device(activations, w_base, blk_vals, blk_index, blk_count, a_down, b_up, grad_out):
        hb, fb = activations.shape
        nsl, rank = blk_vals.shape[0], a_down.shape[1]
        scale = float(hb * nt) ** (-0.5)
        ra, rb = rank // ny, nsl * BLK // nt
        dma = pltpu.SemaphoreType.DMA
        vmem = pltpu.VMEM
        shapes = [
            jax.ShapeDtypeStruct((hb, fb), BF16),
            jax.ShapeDtypeStruct((hb, fb), BF16),
            jax.ShapeDtypeStruct((rank, fb), F32),
            jax.ShapeDtypeStruct((rank, fb), F32),
            jax.ShapeDtypeStruct((nsl * BLK, BLK), F32),
        ]
        results = pl.pallas_call(
            functools.partial(kernel, dims, scale),
            out_shape=shapes,
            in_specs=[pl.BlockSpec(memory_space=pltpu.HBM)] * 8,
            out_specs=[pl.BlockSpec(memory_space=vmem)] * 5,
            scratch_shapes=[
                vmem((hb, fb), BF16), vmem((fb, 2 * fb), BF16), vmem((nsl, BLK, BLK), BF16), vmem((2, nsl), jnp.int32),
                vmem((1, 1), jnp.int32), vmem((rank, fb), BF16), vmem((rank, fb), BF16), vmem((hb, fb), BF16),
                vmem((ny + 1, 2, fb, fb), BF16),
                vmem((nx, nq, 2, fb, fb), BF16),
                vmem((nx, NC * hb, fb), BF16),
                vmem((nq, 2, NC * hb, fb), BF16),
                vmem((nz, hb, fb), BF16),
                vmem((2 * nq, NC * hb, fb), BF16),
                vmem((nx, hb, fb), BF16),
                vmem((nx, hb, fb), BF16),
                vmem((nx, NC * hb, fb), F32),
                vmem((nx, hb, fb), BF16),
                vmem((nx, hb, fb), BF16),
                vmem((nx, hb // nx, 2 * rank), BF16),
                vmem((nx, hb // nx, 2 * rank), BF16),
                vmem((nz, hb // nx, 2 * rank), BF16),
                vmem((nx, hb // nx, 2 * rank), BF16),
                vmem((hb, 2 * rank), BF16),
                vmem((nx, 8, BLK), F32),
                vmem((nx, nsl * BLK, BLK), F32),
                vmem((nx // NC, nsl * BLK, BLK), BF16),
                vmem((nx // NC, nsl * BLK, BLK), BF16),
                vmem((rank, fb), BF16),
                vmem((rank, fb), BF16),
                vmem((nx // NC, NC, rb, BLK), BF16),
                vmem((nx, rb, BLK), BF16),
                vmem((2 * ra + rb, BLK), F32),
                vmem((ny, 2 * ra + nx * rb, BLK), BF16),
                vmem((ny, 2 * ra + nx * rb, BLK), BF16),
                vmem((nt, 2 * ra + rb, BLK), BF16),
                vmem((4, 2 * rank, fb), BF16),
                vmem((2 * rank, fb), F32),
                dma((8,)),
                dma((2, ny)), dma((2, ny)),
                dma((ny + 1, 2)), dma((nx, nq, 2)),
                dma((nx,)),
                dma((nx,)), dma((nx,)),
                dma((nx,)), dma((nx,)),
                dma((nz,)), dma((nq, 2, NC)),
                dma((2 * nq, NC)), dma((nz,)),
                dma((nx,)), dma((nx,)),
                dma((1,)), dma((1,)),
                dma((nx,)), dma((nx,)),
                dma((nz,)), dma((nz,)),
                dma((nx,)), dma((nx,)),
                dma((nx,)), dma((nx,)),
                dma((2,)), dma((2,)),
                dma((nx // NC, NC)), dma((nx,)),
                dma((ny,)), dma((ny,)),
                dma((nt,)), dma((nt,)),
            ],
            compiler_params=pltpu.CompilerParams(
                collective_id=0, has_side_effects=True, vmem_limit_bytes=63 * 1024 * 1024
            ),
        )(activations, w_base, blk_vals, blk_index.T, blk_count.reshape(1, 1), a_down.T, b_up, grad_out)
        proj, gradx, grad_at, grad_b, blk = pl.pallas_call(
            write_out,
            out_shape=shapes,
            in_specs=[pl.BlockSpec(memory_space=pltpu.HBM)] * 5,
            out_specs=[pl.BlockSpec(memory_space=pltpu.HBM)] * 5,
            scratch_shapes=[vmem(s.shape, s.dtype) for s in shapes] + [dma((5,)), dma((5,))],
            compiler_params=pltpu.CompilerParams(vmem_limit_bytes=63 * 1024 * 1024),
        )(*results)
        return proj, gradx, blk.reshape(nsl, BLK, BLK), grad_at.T, grad_b

    return on_device


def solution(mesh, dims=(4, 8, 8)):
    in_specs = (
        P("tok", "feat"),
        P("feat", "tok"),
        P("feat", None, None),
        P("feat", None),
        P("feat"),
        P("feat", None),
        P(None, "feat"),
        P("tok", "feat"),
    )
    out_specs = (
        P("tok", "feat"),
        P("tok", "feat"),
        P("feat", None, None),
        P("feat", None),
        P(None, "feat"),
    )
    return jax.shard_map(make(dims), mesh=mesh, in_specs=in_specs, out_specs=out_specs, check_vma=False)
```
